32 devices in a mesh: nodes: 8 (over z, y), mp: 4 (over x, core).
Axes of the slice: x: 2, y: 2, z: 4, core: 2. Of those that a mesh axis runs over, the one named last changes fastest.
Arguments:
- query: bfloat16 [2048, 512], P('nodes', 'mp'), may hold values from -240 to 240
- key: bfloat16 [2048, 512], P('nodes', 'mp'), may hold values from -7 to 7
- value: bfloat16 [2048, 512], P('nodes', 'mp'), may hold values from -12 to 12
- out_weight: bfloat16 [512, 512], P('mp'), may hold values from -0.25 to 0.25
- cotangent: bfloat16 [2048, 512], P('nodes', 'mp'), may hold values from -6 to 6
- virtual_key: bfloat16 [64, 512], P('nodes', 'mp'), may hold values from -6 to 6
- virtual_value: bfloat16 [64, 512], P('nodes', 'mp'), may hold values from -12 to 12
- halo_rows: int32 [8, 2, 128], P('nodes'), may hold values from 0 to 255
- halo_live: int32 [8, 2], P('nodes'), may hold values from 64 to 128, as said below
- expand_rows: int32 [8, 8, 2], P('nodes'), may hold values from 0 to 255
- local_mask: int32 [16, 4], P('nodes'), may hold values from 0 to 1, as said below
- expand_mask: int32 [16, 8], P('nodes'), may hold values 0 or 1
Outputs:
- output: bfloat16 [2048, 512], P('nodes', 'mp')
- grad_query: float32 [2048, 512], P('nodes', 'mp')
- grad_key: float32 [2048, 512], P('nodes', 'mp')
- grad_value: float32 [2048, 512], P('nodes', 'mp')
- grad_virtual_key: float32 [64, 512], P('nodes', 'mp')
- grad_virtual_value: float32 [64, 512], P('nodes', 'mp')
The draws below stay inside these ranges and needn't reach their ends.
Inputs may be any that keep to these rules, and one draw needn't show every extreme that they name: halo_rows[p, 0, :] index nodes of partition p (0 to 255) sent to partition p + 1, halo_rows[p, 1, :] those sent to partition p - 1; repeats possible. Only the leading halo_live slots of what a partition receives from a neighbour are edges; the value 128 occurs in every draw. expand_rows[r, p, :] index nodes of partition r. Every query tile attends its own tile and both received boundary tiles: local_mask[t, t mod 2], local_mask[t, 2] and local_mask[t, 3] are 1.
All inputs are finite; a program needn't handle non-finite values. No bound on the sum of `expand_mask` on one device may be relied on, other than what follows from the above.
Results may differ from the reference program's by a relative error of at most 0.034.
Values may be sent and summed in bfloat16 or wider, within the bound.
A program may use at most 64 MiB of HBM per device.

```python
import jax
import jax.numpy as jnp
from jax import lax

D = 512
HEADS = 8
NODE_DEV = 256
TILE = 128
HALO_CAP = 128
EXP_SLOT = 2
VN = 64
NODES = 2048
N_NODES = 8


def pair_fields(key):
    key_field = jnp.clip(jax.random.normal(jax.random.fold_in(key, 101), (NODES, D), jnp.float32), -6.0, 6.0)
    query_field = 2.0 * jnp.clip(jax.random.normal(jax.random.fold_in(key, 102), (NODES, D), jnp.float32), -6.0, 6.0)
    return (key_field, query_field)


def draw_query(key, part):
    return pair_fields(key)[1].astype(jnp.bfloat16)


def draw_key(key, part):
    return pair_fields(key)[0].astype(jnp.bfloat16)


def draw_halo_live(key, part):
    devices = NODES // NODE_DEV
    levels = jax.random.randint(jax.random.fold_in(key, 7), (devices, 2), 0, 2)
    live = HALO_CAP // jnp.power(2, levels)
    chosen = jax.random.randint(jax.random.fold_in(key, 8), (), 0, devices * 2)
    flat_index = jnp.arange(devices * 2).reshape(devices, 2)
    return jnp.where(flat_index == chosen, HALO_CAP, live).astype(jnp.int32)


def draw_local_mask(key, part):
    tiles = NODES // TILE
    columns = NODE_DEV // TILE + 2
    random_bits = jax.random.randint(jax.random.fold_in(key, 9), (tiles, columns), 0, 2)
    tile_ids = jnp.arange(tiles)[:, None]
    column_ids = jnp.arange(columns)[None, :]
    forced = (column_ids == tile_ids % (NODE_DEV // TILE)) | (column_ids >= NODE_DEV // TILE)
    return jnp.where(forced, 1, random_bits).astype(jnp.int32)


def set_ends(drawn, stream_key, least, high):
    spot = [jax.random.randint(jax.random.fold_in(stream_key, axis), (), 0, length) for axis, length in enumerate(drawn.shape)]
    longest = drawn.shape.index(max(drawn.shape))
    neighbour = spot[:longest] + [(spot[longest] + 1) % drawn.shape[longest]] + spot[longest + 1:]
    return drawn.at[tuple(spot)].set(least).at[tuple(neighbour)].set(high)


def steps_of(own_key, dims, pieces, smallest, high):
    def one(position, shards_of):
        draws = jax.random.uniform(jax.random.fold_in(jax.random.fold_in(own_key, 6), position), (shards_of,), jnp.float32, smallest / len(pieces), high / len(pieces))
        return jnp.repeat(jnp.exp(draws), dims[position] // shards_of).reshape((-1,) + (1,) * (len(dims) - position - 1))

    level = one(*pieces[0])
    for cut in pieces[1:]:
        level = level * one(*cut)
    return level


def gaussian(own_key, extent, spread, reach, shards=(), held_as=jnp.bfloat16):
    result = jax.random.normal(own_key, extent, jnp.float32) * spread
    if len(shards) > 0:
        result = steps_of(own_key, extent, shards, -0.22, 0.18) * result
    return jnp.clip(result, min=-reach, max=reach).astype(held_as)


def setup_inputs(seed: int = 0) -> dict:
    arg_keys = jax.random.split(jax.random.key(seed), 13)
    query = draw_query(jax.random.fold_in(arg_keys[12], 71), 0)
    key = draw_key(jax.random.fold_in(arg_keys[12], 71), 0)
    value = gaussian(arg_keys[2], (NODES, D), 2.0, 12.0, ((0, 8), (1, 4)))
    out_weight = gaussian(arg_keys[3], (D, D), D ** -0.5, 0.25, ((0, 4),))
    cotangent = gaussian(arg_keys[4], (NODES, D), 1.0, 6.0, ((0, 8), (1, 4)))
    virtual_key = gaussian(arg_keys[5], (VN, D), 1.0, 6.0, ((0, 8), (1, 4)))
    virtual_value = gaussian(arg_keys[6], (VN, D), 2.0, 12.0, ((0, 8), (1, 4)))
    halo_rows = set_ends(jax.random.randint(arg_keys[7], (N_NODES, 2, HALO_CAP), 0, NODE_DEV), jax.random.fold_in(arg_keys[7], 1), 0, NODE_DEV - 1).astype(jnp.int32)
    halo_live = draw_halo_live(jax.random.fold_in(arg_keys[12], 71), 0)
    expand_rows = set_ends(jax.random.randint(arg_keys[9], (N_NODES, N_NODES, EXP_SLOT), 0, NODE_DEV), jax.random.fold_in(arg_keys[9], 1), 0, NODE_DEV - 1).astype(jnp.int32)
    local_mask = draw_local_mask(jax.random.fold_in(arg_keys[12], 71), 0)
    expand_mask = set_ends((jax.random.randint(arg_keys[11], (NODES // TILE, N_NODES), 0, 4) < 1).astype(jnp.int32), jax.random.fold_in(arg_keys[11], 1), 0, 1)
    return {"query": query, "key": key, "value": value, "out_weight": out_weight, "cotangent": cotangent, "virtual_key": virtual_key, "virtual_value": virtual_value, "halo_rows": halo_rows, "halo_live": halo_live, "expand_rows": expand_rows, "local_mask": local_mask, "expand_mask": expand_mask}


def edge_mask(local_block, expand_block, live, tile_rows, halo_cap, exp_slot, virtual_count):
    tile_count = local_block.shape[0]
    own_tiles = jnp.repeat(jnp.repeat(local_block[:, :tile_count] > 0, tile_rows, axis=0), tile_rows, axis=1)
    slot_index = jnp.arange(halo_cap)
    left_ok = (local_block[:, tile_count] > 0)[:, None] & (slot_index < live[0])[None, :]
    right_ok = (local_block[:, tile_count + 1] > 0)[:, None] & (slot_index < live[1])[None, :]
    expand_ok = jnp.repeat(expand_block > 0, exp_slot, axis=1)
    remote_tiles = jnp.repeat(jnp.concatenate([left_ok, right_ok, expand_ok], axis=1), tile_rows, axis=0)
    virtual_ok = jnp.ones((tile_count * tile_rows, virtual_count), dtype=jnp.bool_)
    return jnp.concatenate([own_tiles, remote_tiles, virtual_ok], axis=1)


def reference(query, key, value, out_weight, cotangent, virtual_key, virtual_value, halo_rows, halo_live, expand_rows, local_mask, expand_mask):
    node_rows = NODE_DEV
    part_count = N_NODES
    tile_count = NODE_DEV // TILE
    head_dim = D // HEADS
    score_scale = head_dim ** -0.5
    part_ids = jnp.arange(part_count, dtype=jnp.int32)
    left_part = (part_ids - 1) % part_count
    right_part = (part_ids + 1) % part_count
    left_index = left_part[:, None] * node_rows + halo_rows[left_part, 0]
    right_index = right_part[:, None] * node_rows + halo_rows[right_part, 1]
    expand_index = (part_ids[:, None, None] * node_rows + expand_rows).transpose(1, 0, 2).reshape(part_count, part_count * EXP_SLOT)
    own_index = part_ids[:, None] * node_rows + jnp.arange(node_rows, dtype=jnp.int32)[None, :]
    key_index = jnp.concatenate([own_index, left_index, right_index, expand_index], axis=1).astype(jnp.int32)
    local_keys = key_index.shape[1]

    def block_step(carry, part):
        grad_key_all, grad_value_all, virtual_key_grad, virtual_value_grad = carry
        row_start = (part * node_rows).astype(jnp.int32)
        tile_start = (part * tile_count).astype(jnp.int32)
        block_query = lax.dynamic_slice_in_dim(query, row_start, node_rows, 0)
        block_cot = lax.dynamic_slice_in_dim(cotangent, row_start, node_rows, 0)
        block_local = lax.dynamic_slice_in_dim(local_mask, tile_start, tile_count, 0)
        block_expand = lax.dynamic_slice_in_dim(expand_mask, tile_start, tile_count, 0)
        gather_index = key_index[part]
        all_keys = jnp.concatenate([key[gather_index], virtual_key], axis=0)
        all_values = jnp.concatenate([value[gather_index], virtual_value], axis=0)
        key_total = all_keys.shape[0]
        allowed = edge_mask(block_local, block_expand, halo_live[part], TILE, HALO_CAP, EXP_SLOT, VN)
        query_heads = block_query.astype(jnp.float32).reshape(node_rows, HEADS, head_dim)
        key_heads = all_keys.astype(jnp.float32).reshape(key_total, HEADS, head_dim)
        value_heads = all_values.astype(jnp.float32).reshape(key_total, HEADS, head_dim)
        scores = jnp.einsum('qhd,khd->hqk', query_heads, key_heads) * score_scale
        scores = jnp.where(allowed[None], scores, -1e30)
        row_max = jnp.max(scores, axis=-1, keepdims=True)
        weights = jnp.exp(scores - row_max)
        probs = weights / jnp.sum(weights, axis=-1, keepdims=True)
        probs_b = lax.optimization_barrier(probs.astype(jnp.bfloat16)).astype(jnp.float32)
        attn = jnp.einsum('hqk,khd->qhd', probs_b, value_heads).astype(jnp.bfloat16).reshape(node_rows, D)
        output_block = jnp.dot(attn, out_weight, preferred_element_type=jnp.float32).astype(jnp.bfloat16)
        d_attn = jnp.dot(block_cot, out_weight.T, preferred_element_type=jnp.float32).astype(jnp.bfloat16)
        grad_heads = d_attn.astype(jnp.float32).reshape(node_rows, HEADS, head_dim)
        attn_heads = attn.astype(jnp.float32).reshape(node_rows, HEADS, head_dim)
        row_delta = jnp.sum(grad_heads * attn_heads, axis=-1).transpose(1, 0)[:, :, None]
        d_prob = jnp.einsum('qhd,khd->hqk', grad_heads, value_heads)
        d_score = lax.optimization_barrier((probs * (d_prob - row_delta) * score_scale).astype(jnp.bfloat16)).astype(jnp.float32)
        grad_query_block = jnp.einsum('hqk,khd->qhd', d_score, key_heads).reshape(node_rows, D)
        grad_keys = jnp.einsum('hqk,qhd->khd', d_score, query_heads).reshape(key_total, D)
        grad_values = jnp.einsum('hqk,qhd->khd', probs_b, grad_heads).reshape(key_total, D)
        grad_key_all = grad_key_all.at[gather_index].add(grad_keys[:local_keys])
        grad_value_all = grad_value_all.at[gather_index].add(grad_values[:local_keys])
        virtual_key_grad = virtual_key_grad + grad_keys[local_keys:]
        virtual_value_grad = virtual_value_grad + grad_values[local_keys:]
        return (grad_key_all, grad_value_all, virtual_key_grad, virtual_value_grad), (output_block, grad_query_block)

    start_carry = (jnp.zeros((NODES, D), jnp.float32), jnp.zeros((NODES, D), jnp.float32), jnp.zeros((VN, D), jnp.float32), jnp.zeros((VN, D), jnp.float32))
    final_carry, stacked = lax.scan(block_step, start_carry, part_ids)
    grad_key_all, grad_value_all, virtual_key_grad, virtual_value_grad = final_carry
    output = stacked[0].reshape(NODES, D)
    grad_query = stacked[1].reshape(NODES, D)
    return (output, grad_query, grad_key_all, grad_value_all, virtual_key_grad, virtual_value_grad)
```

```python
import functools

import jax
import jax.numpy as jnp
from jax import lax
from jax.experimental import pallas as pl
from jax.experimental.pallas import tpu as pltpu
from jax.sharding import PartitionSpec as P

HEADS = 8
MESH = pl.DeviceIdType.MESH
BF = jnp.bfloat16
F32 = jnp.float32
MASKED = -1e30

NN = (((1,), (0,)), ((), ()))
NT = (((1,), (1,)), ((), ()))
TN = (((0,), (0,)), ((), ()))


def mm(a, b, dims):
    return lax.dot_general(a, b, dims, preferred_element_type=F32)


def iota(shape, axis):
    return lax.broadcasted_iota(jnp.int32, shape, axis)


def each(count, step):
    if count <= 8:
        for d in range(count):
            step(d)
    else:
        pl.loop(0, count)(step)


def kernel(
    n, mp, heads,
    live, erows, lmask, emask,
    q_hbm, k_hbm, v_hbm, w_hbm, cot_hbm, vk_hbm, vv_hbm, hrows_hbm,
    out_hbm, gq_hbm, gk_hbm, gv_hbm, gvk_hbm, gvv_hbm,
    q_v, w_v, vk_v, vv_v, hrows, kv, cot, bias, onehot, mix_send, halo_send,
    e_ref, pb_ref, ds_ref, gback, ret_halo, ret_mix, proj, proj_in, own_v,
    out_v, gq_v, gk_v, gv_v, gvk_v, gvv_v,
    in_sem, out_sem, halo_s, halo_r, mix_s, mix_r, cot_s, cot_r, proj_s, proj_r,
    hb_s, hb_r, mb_s, mb_r,
):
    me = lax.axis_index("nodes")
    mm_i = lax.axis_index("mp")
    rows, width = q_v.shape
    tiles = lmask.shape[0]
    tile = rows // tiles
    cap = hrows.shape[2]
    slots = erows.shape[2]
    vn = vk_v.shape[0]
    blk = ret_mix.shape[0] // n
    hd = width // heads
    cols = heads * rows
    left, right = lax.rem(me + n - 1, n), lax.rem(me + 1, n)
    mix0 = rows + 2 * cap
    total = mix0 + n * blk

    barrier = pltpu.get_barrier_semaphore()

    def hello(d):
        pl.semaphore_signal(
            barrier, inc=1, device_id={"nodes": lax.rem(me + d + 1, n)}, device_id_type=MESH
        )

    each(n - 1, hello)
    for d in range(1, mp):
        pl.semaphore_signal(
            barrier, inc=1, device_id={"mp": lax.rem(mm_i + d, mp)}, device_id_type=MESH
        )

    loads = [
        pltpu.make_async_copy(k_hbm, kv.at[:rows, :width], in_sem.at[0]),
        pltpu.make_async_copy(v_hbm, kv.at[:rows, width:], in_sem.at[1]),
        pltpu.make_async_copy(hrows_hbm, hrows, in_sem.at[2]),
        pltpu.make_async_copy(vk_hbm, vk_v, in_sem.at[3]),
        pltpu.make_async_copy(vv_hbm, vv_v, in_sem.at[4]),
        pltpu.make_async_copy(cot_hbm, cot.at[mm_i], in_sem.at[5]),
        pltpu.make_async_copy(q_hbm, q_v, in_sem.at[6]),
        pltpu.make_async_copy(w_hbm, w_v, in_sem.at[7]),
    ]
    for c in loads:
        c.start()

    row_b, lane_b = iota((blk, rows), 0), iota((blk, rows), 1)

    def fill(d):
        peer = lax.rem(me + d, n)
        target = jnp.full((blk, rows), -1, jnp.int32)
        for s in range(slots):
            target = jnp.where(row_b == vn + s, erows[0, peer, s], target)
        onehot[pl.ds(d * blk, blk), :] = jnp.where(lane_b == target, 1.0, 0.0).astype(BF)

    each(n, fill)

    for c in loads[:5]:
        c.wait()
    own = kv[:rows, :]
    g_right = jnp.where(iota((rows, cap), 0) == hrows[0, 0:1, :], 1.0, 0.0).astype(BF)
    g_left = jnp.where(iota((rows, cap), 0) == hrows[0, 1:2, :], 1.0, 0.0).astype(BF)
    halo_send[0] = mm(g_right, own, TN).astype(BF)
    halo_send[1] = mm(g_left, own, TN).astype(BF)
    virt = jnp.concatenate([vk_v[...].astype(F32), vv_v[...].astype(F32)], axis=1)
    virt = jnp.concatenate([virt, jnp.zeros((blk - vn, 2 * width), F32)], axis=0)
    taken = mm(onehot[...], own, NN).reshape(n, blk, 2 * width) + virt[None]
    taken = taken.astype(BF)
    mix_send[...] = taken.reshape(n * blk, 2 * width)
    kv[mix0 : mix0 + blk, :] = taken[0]
    loads[5].wait()

    pl.semaphore_wait(barrier, n - 1 + mp - 1)

    def halo_copy(side):
        start = rows + side * cap
        return pltpu.make_async_remote_copy(
            halo_send.at[side], kv.at[start : start + cap, :], halo_s.at[side], halo_r.at[side],
            device_id={"nodes": right if side == 0 else left}, device_id_type=MESH,
        )

    def mix_copy(d):
        return pltpu.make_async_remote_copy(
            mix_send.at[pl.ds(d * blk, blk), :], kv.at[pl.ds(mix0 + d * blk, blk), :],
            mix_s.at[d], mix_r.at[d],
            device_id={"nodes": lax.rem(me + d, n)}, device_id_type=MESH,
        )

    def cot_copy(d, slot):
        return pltpu.make_async_remote_copy(
            cot.at[slot], cot.at[slot], cot_s.at[d], cot_r.at[d],
            device_id={"mp": lax.rem(mm_i + d, mp)}, device_id_type=MESH,
        )

    halo = [halo_copy(0), halo_copy(1)]
    for c in halo:
        c.start()
    each(n - 1, lambda d: mix_copy(d + 1).start())
    for d in range(1, mp):
        cot_copy(d, mm_i).start()

    lane = iota((1, width), 1)

    def per_tile(values):
        result = jnp.zeros(values[0].shape, F32)
        for t in range(tiles):
            result = jnp.where(lane == t, values[t], result)
        return result.astype(BF)

    def flag(x):
        return jnp.where(x > 0, 0.0, MASKED)

    for u in range(tiles):
        bias[u * tile : (u + 1) * tile, :] = per_tile(
            [jnp.full((tile, width), flag(lmask[t, u]), F32) for t in range(tiles)]
        )
    row_c = iota((cap, width), 0)
    for side in range(2):
        start = rows + side * cap
        bias[start : start + cap, :] = per_tile(
            [
                jnp.where(row_c < live[0, side], flag(lmask[t, tiles + side]), MASKED)
                for t in range(tiles)
            ]
        )
    row_m = iota((blk, width), 0)

    def mix_mask(d):
        source = lax.rem(me + n - d, n)
        values = []
        for t in range(tiles):
            inner = jnp.where(row_m < vn + slots, flag(emask[t, source]), MASKED)
            values.append(jnp.where(row_m < vn, 0.0, inner))
        bias[pl.ds(mix0 + d * blk, blk), :] = per_tile(values)

    each(n, mix_mask)

    feature = iota((width, rows), 0)

    def blocks(x):
        parts = []
        for h in range(heads):
            mine = (feature >= h * hd) & (feature < (h + 1) * hd)
            parts.append(jnp.where(mine, x, 0.0))
        return jnp.concatenate(parts, axis=1).astype(BF)

    loads[6].wait()
    q_t = jnp.transpose(q_v[...].astype(F32)) * (hd ** -0.5)
    q_blocks = blocks(q_t)
    col = iota((width, cols), 1)
    for h in range(1, heads):
        col = jnp.where(iota((width, cols), 1) >= h * rows, iota((width, cols), 1) - h * rows, col)
    tile_of = jnp.zeros((width, cols), jnp.int32)
    for t in range(1, tiles):
        tile_of = jnp.where(col >= t * tile, t, tile_of)
    in_tile = jnp.where(iota((width, cols), 0) == tile_of, 1.0, 0.0).astype(BF)
    q_aug = jnp.concatenate([q_blocks, in_tile], axis=0)

    chunks = [(0, rows), (rows, 2 * cap)]
    step_rows = min(n * blk, 256)
    chunks += [(mix0 + i, step_rows) for i in range(0, n * blk, step_rows)]

    def score(c):
        a, size = c
        keys = jnp.concatenate([kv[a : a + size, :width], bias[a : a + size, :]], axis=1)
        s = mm(keys, q_aug, NN)
        e_ref[a : a + size, :] = s
        return jnp.max(s, axis=0, keepdims=True)

    top = score(chunks[0])

    loads[7].wait()
    for d in range(1, mp):
        cot_copy(d, lax.rem(mm_i + mp - d, mp)).wait_recv()
    g_t = mm(w_v[...], jnp.concatenate([cot[i] for i in range(mp)], axis=1), NT)
    g_t = g_t.astype(BF).astype(F32)
    g_blocks = blocks(g_t)

    for c in halo:
        c.wait_recv()
    top = jnp.maximum(top, score(chunks[1]))
    each(n - 1, lambda d: mix_copy(d + 1).wait_recv())
    for c in chunks[2:]:
        top = jnp.maximum(top, score(c))

    norm = jnp.zeros((1, cols), F32)
    for a, size in chunks:
        e = jnp.exp(e_ref[a : a + size, :] - top)
        e_ref[a : a + size, :] = e
        norm = norm + jnp.sum(e, axis=0, keepdims=True)
    inv = 1.0 / norm
    for a, size in chunks:
        p = e_ref[a : a + size, :] * inv
        e_ref[a : a + size, :] = p
        pb_ref[a : a + size, :] = p.astype(BF)

    v_t = jnp.transpose(kv[:, width:])
    attn_t = jnp.concatenate(
        [
            mm(v_t[h * hd : (h + 1) * hd, :], pb_ref[:, h * rows : (h + 1) * rows], NN)
            for h in range(heads)
        ],
        axis=0,
    )
    attn_t = attn_t.astype(BF).astype(F32)
    prod = g_t * attn_t
    delta = jnp.concatenate(
        [jnp.sum(prod[h * hd : (h + 1) * hd, :], axis=0, keepdims=True) for h in range(heads)],
        axis=1,
    )
    attn = jnp.transpose(attn_t).astype(BF)

    def proj_copy(d):
        peer = lax.rem(mm_i + d, mp)
        return pltpu.make_async_remote_copy(
            proj.at[peer], proj_in.at[d], proj_s.at[d], proj_r.at[d],
            device_id={"mp": peer}, device_id_type=MESH,
        )

    full = mm(attn, w_v[...], NN)
    for i in range(mp):
        proj[i] = full[:, i * width : (i + 1) * width].astype(BF)
    for d in range(1, mp):
        proj_copy(d).start()
    mine = mm(attn, w_v[:, pl.ds(pl.multiple_of(mm_i * width, width), width)], NN)

    def backward(c):
        a, size = c
        dp = mm(kv[a : a + size, width:], g_blocks, NN)
        ds = (e_ref[a : a + size, :] * (dp - delta)).astype(BF)
        ds_ref[a : a + size, :] = ds
        gk = mm(ds, q_blocks, NT)
        gv = mm(pb_ref[a : a + size, :], g_blocks, NT)
        return gk, gv

    def halo_home(side):
        return pltpu.make_async_remote_copy(
            gback.at[side * cap : (side + 1) * cap, :], ret_halo.at[side],
            hb_s.at[side], hb_r.at[side],
            device_id={"nodes": left if side == 0 else right}, device_id_type=MESH,
        )

    def mix_home(d):
        return pltpu.make_async_remote_copy(
            gback.at[pl.ds(2 * cap + d * blk, blk), :], ret_mix.at[pl.ds(d * blk, blk), :],
            mb_s.at[d], mb_r.at[d],
            device_id={"nodes": lax.rem(me + n - d, n)}, device_id_type=MESH,
        )

    gk, gv = backward(chunks[1])
    gback[: 2 * cap, :width] = gk.astype(BF)
    gback[: 2 * cap, width:] = gv.astype(BF)
    home = [halo_home(0), halo_home(1)]
    for c in home:
        c.start()
    for c in chunks[2:]:
        gk, gv = backward(c)
        a = c[0] - rows
        gback[a : a + c[1], :width] = gk.astype(BF)
        gback[a : a + c[1], width:] = gv.astype(BF)
    each(n - 1, lambda d: mix_home(d + 1).start())
    gk, gv = backward(chunks[0])
    own_v[:, :width] = gk
    own_v[:, width:] = gv
    ret_mix[:blk, :] = gback[2 * cap : 2 * cap + blk, :]

    k_t = jnp.transpose(kv[:, :width])
    gq_t = jnp.concatenate(
        [
            mm(k_t[h * hd : (h + 1) * hd, :], ds_ref[:, h * rows : (h + 1) * rows], NN)
            for h in range(heads)
        ],
        axis=0,
    )
    gq_v[...] = jnp.transpose(gq_t * (hd ** -0.5))
    stores = [pltpu.make_async_copy(gq_v, gq_hbm, out_sem.at[0])]
    stores[-1].start()

    for d in range(1, mp):
        proj_copy(d).wait_recv()
        mine = mine + proj_in[d].astype(F32)
    out_v[...] = mine.astype(BF)
    stores.append(pltpu.make_async_copy(out_v, out_hbm, out_sem.at[1]))
    stores[-1].start()

    for c in home:
        c.wait_recv()
    acc = own_v[...] + mm(g_right, ret_halo[0], NN) + mm(g_left, ret_halo[1], NN)
    each(n - 1, lambda d: mix_home(d + 1).wait_recv())
    acc = acc + mm(onehot[...], ret_mix[...], TN)
    gk_v[...] = acc[:, :width]
    gv_v[...] = acc[:, width:]
    virt = jnp.sum(ret_mix[...].astype(F32).reshape(n, blk, 2 * width), axis=0)
    gvk_v[...] = virt[:vn, :width]
    gvv_v[...] = virt[:vn, width:]
    for i, (src, dst) in enumerate(
        ((gk_v, gk_hbm), (gv_v, gv_hbm), (gvk_v, gvk_hbm), (gvv_v, gvv_hbm))
    ):
        stores.append(pltpu.make_async_copy(src, dst, out_sem.at[2 + i]))
        stores[-1].start()

    for c in halo + home:
        c.wait_send()
    each(n - 1, lambda d: mix_copy(d + 1).wait_send())
    each(n - 1, lambda d: mix_home(d + 1).wait_send())
    for d in range(1, mp):
        cot_copy(d, mm_i).wait_send()
        proj_copy(d).wait_send()
    for c in stores:
        c.wait()


def solution(mesh):
    n, mp = mesh.shape["nodes"], mesh.shape["mp"]
    heads = HEADS // mp

    def step(q, k, v, w, cot, vk, vv, hrows, live, erows, lmask, emask):
        rows, width = q.shape
        cap, slots, vn = hrows.shape[2], erows.shape[2], vk.shape[0]
        blk = -(-(vn + slots) // 16) * 16
        total = rows + 2 * cap + n * blk
        smem = pl.BlockSpec(memory_space=pltpu.SMEM)
        hbm = pl.BlockSpec(memory_space=pl.ANY)
        dma = pltpu.SemaphoreType.DMA
        flops = 2 * total * rows * width * 5
        return pl.pallas_call(
            functools.partial(kernel, n, mp, heads),
            out_shape=(
                jax.ShapeDtypeStruct((rows, width), BF),
                jax.ShapeDtypeStruct((rows, width), F32),
                jax.ShapeDtypeStruct((rows, width), F32),
                jax.ShapeDtypeStruct((rows, width), F32),
                jax.ShapeDtypeStruct((vn, width), F32),
                jax.ShapeDtypeStruct((vn, width), F32),
            ),
            in_specs=[smem] * 4 + [hbm] * 8,
            out_specs=(hbm,) * 6,
            scratch_shapes=[
                pltpu.VMEM((rows, width), BF),
                pltpu.VMEM(w.shape, BF),
                pltpu.VMEM((vn, width), BF),
                pltpu.VMEM((vn, width), BF),
                pltpu.VMEM(hrows.shape, jnp.int32),
                pltpu.VMEM((total, 2 * width), BF),
                pltpu.VMEM((mp, rows, width), BF),
                pltpu.VMEM((total, width), BF),
                pltpu.VMEM((n * blk, rows), BF),
                pltpu.VMEM((n * blk, 2 * width), BF),
                pltpu.VMEM((2, cap, 2 * width), BF),
                pltpu.VMEM((total, heads * rows), F32),
                pltpu.VMEM((total, heads * rows), BF),
                pltpu.VMEM((total, heads * rows), BF),
                pltpu.VMEM((2 * cap + n * blk, 2 * width), BF),
                pltpu.VMEM((2, cap, 2 * width), BF),
                pltpu.VMEM((n * blk, 2 * width), BF),
                pltpu.VMEM((mp, rows, width), BF),
                pltpu.VMEM((mp, rows, width), BF),
                pltpu.VMEM((rows, 2 * width), F32),
                pltpu.VMEM((rows, width), BF),
                pltpu.VMEM((rows, width), F32),
                pltpu.VMEM((rows, width), F32),
                pltpu.VMEM((rows, width), F32),
                pltpu.VMEM((vn, width), F32),
                pltpu.VMEM((vn, width), F32),
                dma((8,)), dma((6,)),
                dma((2,)), dma((2,)), dma((n,)), dma((n,)),
                dma((mp,)), dma((mp,)), dma((mp,)), dma((mp,)),
                dma((2,)), dma((2,)), dma((n,)), dma((n,)),
            ],
            compiler_params=pltpu.CompilerParams(
                collective_id=0, has_side_effects=True, vmem_limit_bytes=48 << 20
            ),
            cost_estimate=pl.CostEstimate(
                flops=flops, transcendentals=total * rows * heads, bytes_accessed=2 << 20
            ),
        )(live, erows, lmask, emask, q, k, v, w, cot, vk, vv, hrows)

    node = P("nodes", "mp")
    return jax.shard_map(
        step,
        mesh=mesh,
        in_specs=(
            node, node, node, P("mp", None), node, node, node,
            P("nodes", None, None), P("nodes", None), P("nodes", None, None),
            P("nodes", None), P("nodes", None),
        ),
        out_specs=(node,) * 6,
        check_vma=False,
    )
```

```python
import functools

import jax
import jax.numpy as jnp
from jax import lax
from jax.experimental import pallas as pl
from jax.experimental.pallas import tpu as pltpu
from jax.sharding import PartitionSpec as P

HEADS = 8
MESH = pl.DeviceIdType.MESH
BF = jnp.bfloat16
F32 = jnp.float32
MASKED = -1e30

NN = (((1,), (0,)), ((), ()))
NT = (((1,), (1,)), ((), ()))
TN = (((0,), (0,)), ((), ()))


def mm(a, b, dims):
    return lax.dot_general(a, b, dims, preferred_element_type=F32)


def iota(shape, axis):
    return lax.broadcasted_iota(jnp.int32, shape, axis)


def each(count, step):
    if count <= 8:
        for d in range(count):
            step(d)
    else:
        pl.loop(0, count)(step)


def kernel(
    n, mp, heads,
    live_hbm, erows_hbm, lmask_hbm, emask_hbm,
    q_hbm, k_hbm, v_hbm, w_hbm, cot_hbm, vk_hbm, vv_hbm, hrows_hbm,
    out_hbm, gq_hbm, gk_hbm, gv_hbm, gvk_hbm, gvv_hbm,
    live, erows, lmask, emask, q_v, w_v, vk_v, vv_v, hrows, kv, cot, bias, onehot, mix_send, halo_send,
    e_ref, pb_ref, ds_ref, gback, ret_halo, ret_mix, proj, proj_in, own_v,
    out_v, gq_v, gk_v, gv_v, gvk_v, gvv_v,
    in_sem, out_sem, halo_s, halo_r, mix_s, mix_r, cot_s, cot_r, proj_s, proj_r,
    hb_s, hb_r, mb_s, mb_r,
):
    me = lax.axis_index("nodes")
    mm_i = lax.axis_index("mp")
    rows, width = q_v.shape
    tiles = lmask.shape[0]
    tile = rows // tiles
    cap = hrows.shape[2]
    slots = erows.shape[1]
    vn = vk_v.shape[0]
    blk = ret_mix.shape[0] // n
    hd = width // heads
    cols = heads * rows
    left, right = lax.rem(me + n - 1, n), lax.rem(me + 1, n)
    mix0 = rows + 2 * cap
    total = mix0 + n * blk

    barrier = pltpu.get_barrier_semaphore()

    def hello(d):
        pl.semaphore_signal(
            barrier, inc=1, device_id={"nodes": lax.rem(me + d + 1, n)}, device_id_type=MESH
        )

    each(n - 1, hello)
    for d in range(1, mp):
        pl.semaphore_signal(
            barrier, inc=1, device_id={"mp": lax.rem(mm_i + d, mp)}, device_id_type=MESH
        )

    small = [
        pltpu.make_async_copy(src, dst, in_sem.at[8 + i])
        for i, (src, dst) in enumerate(
            ((erows_hbm, erows), (live_hbm, live), (lmask_hbm, lmask), (emask_hbm, emask))
        )
    ]
    for c in small:
        c.start()
    loads = [
        pltpu.make_async_copy(k_hbm, kv.at[:rows, :width], in_sem.at[0]),
        pltpu.make_async_copy(v_hbm, kv.at[:rows, width:], in_sem.at[1]),
        pltpu.make_async_copy(hrows_hbm, hrows, in_sem.at[2]),
        pltpu.make_async_copy(vk_hbm, vk_v, in_sem.at[3]),
        pltpu.make_async_copy(vv_hbm, vv_v, in_sem.at[4]),
        pltpu.make_async_copy(cot_hbm, cot.at[mm_i], in_sem.at[5]),
        pltpu.make_async_copy(q_hbm, q_v, in_sem.at[6]),
        pltpu.make_async_copy(w_hbm, w_v, in_sem.at[7]),
    ]
    for c in loads:
        c.start()

    row_b, lane_b = iota((blk, rows), 0), iota((blk, rows), 1)

    def fill(d):
        peer = lax.rem(me + d, n)
        target = jnp.full((blk, rows), -1, jnp.int32)
        for s in range(slots):
            target = jnp.where(row_b == vn + s, erows[0, s, peer], target)
        onehot[pl.ds(d * blk, blk), :] = jnp.where(lane_b == target, 1.0, 0.0).astype(BF)

    small[0].wait()
    each(n, fill)

    for c in loads[:5]:
        c.wait()
    own = kv[:rows, :]
    g_right = jnp.where(iota((rows, cap), 0) == hrows[0, 0:1, :], 1.0, 0.0).astype(BF)
    g_left = jnp.where(iota((rows, cap), 0) == hrows[0, 1:2, :], 1.0, 0.0).astype(BF)
    halo_send[0] = mm(g_right, own, TN).astype(BF)
    halo_send[1] = mm(g_left, own, TN).astype(BF)
    virt = jnp.concatenate([vk_v[...].astype(F32), vv_v[...].astype(F32)], axis=1)
    virt = jnp.concatenate([virt, jnp.zeros((blk - vn, 2 * width), F32)], axis=0)
    taken = mm(onehot[...], own, NN).reshape(n, blk, 2 * width) + virt[None]
    taken = taken.astype(BF)
    mix_send[...] = taken.reshape(n * blk, 2 * width)
    kv[mix0 : mix0 + blk, :] = taken[0]
    loads[5].wait()

    pl.semaphore_wait(barrier, n - 1 + mp - 1)

    def halo_copy(side):
        start = rows + side * cap
        return pltpu.make_async_remote_copy(
            halo_send.at[side], kv.at[start : start + cap, :], halo_s.at[side], halo_r.at[side],
            device_id={"nodes": right if side == 0 else left}, device_id_type=MESH,
        )

    def mix_copy(d):
        return pltpu.make_async_remote_copy(
            mix_send.at[pl.ds(d * blk, blk), :], kv.at[pl.ds(mix0 + d * blk, blk), :],
            mix_s.at[d], mix_r.at[d],
            device_id={"nodes": lax.rem(me + d, n)}, device_id_type=MESH,
        )

    def cot_copy(d, slot):
        return pltpu.make_async_remote_copy(
            cot.at[slot], cot.at[slot], cot_s.at[d], cot_r.at[d],
            device_id={"mp": lax.rem(mm_i + d, mp)}, device_id_type=MESH,
        )

    halo = [halo_copy(0), halo_copy(1)]
    for c in halo:
        c.start()
    each(n - 1, lambda d: mix_copy(d + 1).start())
    for d in range(1, mp):
        cot_copy(d, mm_i).start()

    for c in small[1:]:
        c.wait()

    lane = iota((1, width), 1)

    def per_tile(values):
        result = jnp.zeros(values[0].shape, F32)
        for t in range(tiles):
            result = jnp.where(lane == t, values[t], result)
        return result.astype(BF)

    def flag(x):
        return jnp.where(x > 0, 0.0, MASKED)

    for u in range(tiles):
        bias[u * tile : (u + 1) * tile, :] = per_tile(
            [jnp.full((tile, width), flag(lmask[t, u]), F32) for t in range(tiles)]
        )
    row_c = iota((cap, width), 0)
    for side in range(2):
        start = rows + side * cap
        bias[start : start + cap, :] = per_tile(
            [
                jnp.where(row_c < live[0, side], flag(lmask[t, tiles + side]), MASKED)
                for t in range(tiles)
            ]
        )
    row_m = iota((blk, width), 0)

    def mix_mask(d):
        source = lax.rem(me + n - d, n)
        values = []
        for t in range(tiles):
            inner = jnp.where(row_m < vn + slots, flag(emask[t, source]), MASKED)
            values.append(jnp.where(row_m < vn, 0.0, inner))
        bias[pl.ds(mix0 + d * blk, blk), :] = per_tile(values)

    each(n, mix_mask)

    feature = iota((width, rows), 0)

    def blocks(x):
        parts = []
        for h in range(heads):
            mine = (feature >= h * hd) & (feature < (h + 1) * hd)
            parts.append(jnp.where(mine, x, 0.0))
        return jnp.concatenate(parts, axis=1).astype(BF)

    loads[6].wait()
    q_t = jnp.transpose(q_v[...].astype(F32)) * (hd ** -0.5)
    q_blocks = blocks(q_t)
    col = iota((width, cols), 1)
    for h in range(1, heads):
        col = jnp.where(iota((width, cols), 1) >= h * rows, iota((width, cols), 1) - h * rows, col)
    tile_of = jnp.zeros((width, cols), jnp.int32)
    for t in range(1, tiles):
        tile_of = jnp.where(col >= t * tile, t, tile_of)
    in_tile = jnp.where(iota((width, cols), 0) == tile_of, 1.0, 0.0).astype(BF)
    q_aug = jnp.concatenate([q_blocks, in_tile], axis=0)

    chunks = [(0, rows), (rows, 2 * cap)]
    step_rows = min(n * blk, 256)
    chunks += [(mix0 + i, step_rows) for i in range(0, n * blk, step_rows)]

    def score(c):
        a, size = c
        keys = jnp.concatenate([kv[a : a + size, :width], bias[a : a + size, :]], axis=1)
        s = mm(keys, q_aug, NN)
        e_ref[a : a + size, :] = s
        return jnp.max(s, axis=0, keepdims=True)

    top = score(chunks[0])

    loads[7].wait()
    for d in range(1, mp):
        cot_copy(d, lax.rem(mm_i + mp - d, mp)).wait_recv()
    g_t = mm(w_v[...], jnp.concatenate([cot[i] for i in range(mp)], axis=1), NT)
    g_t = g_t.astype(BF).astype(F32)
    g_blocks = blocks(g_t)

    for c in halo:
        c.wait_recv()
    top = jnp.maximum(top, score(chunks[1]))
    each(n - 1, lambda d: mix_copy(d + 1).wait_recv())
    for c in chunks[2:]:
        top = jnp.maximum(top, score(c))

    norm = jnp.zeros((1, cols), F32)
    for a, size in chunks:
        e = jnp.exp(e_ref[a : a + size, :] - top)
        e_ref[a : a + size, :] = e
        norm = norm + jnp.sum(e, axis=0, keepdims=True)
    inv = 1.0 / norm
    for a, size in chunks:
        p = e_ref[a : a + size, :] * inv
        e_ref[a : a + size, :] = p
        pb_ref[a : a + size, :] = p.astype(BF)

    v_t = jnp.transpose(kv[:, width:])
    attn_t = jnp.concatenate(
        [
            mm(v_t[h * hd : (h + 1) * hd, :], pb_ref[:, h * rows : (h + 1) * rows], NN)
            for h in range(heads)
        ],
        axis=0,
    )
    attn_t = attn_t.astype(BF).astype(F32)
    prod = g_t * attn_t
    delta = jnp.concatenate(
        [jnp.sum(prod[h * hd : (h + 1) * hd, :], axis=0, keepdims=True) for h in range(heads)],
        axis=1,
    )
    attn = jnp.transpose(attn_t).astype(BF)

    def proj_copy(d):
        peer = lax.rem(mm_i + d, mp)
        return pltpu.make_async_remote_copy(
            proj.at[peer], proj_in.at[d], proj_s.at[d], proj_r.at[d],
            device_id={"mp": peer}, device_id_type=MESH,
        )

    full = mm(attn, w_v[...], NN)
    for i in range(mp):
        proj[i] = full[:, i * width : (i + 1) * width].astype(BF)
    for d in range(1, mp):
        proj_copy(d).start()
    mine = mm(attn, w_v[:, pl.ds(pl.multiple_of(mm_i * width, width), width)], NN)

    def backward(c):
        a, size = c
        dp = mm(kv[a : a + size, width:], g_blocks, NN)
        ds = (e_ref[a : a + size, :] * (dp - delta)).astype(BF)
        ds_ref[a : a + size, :] = ds
        gk = mm(ds, q_blocks, NT)
        gv = mm(pb_ref[a : a + size, :], g_blocks, NT)
        return gk, gv

    def halo_home(side):
        return pltpu.make_async_remote_copy(
            gback.at[side * cap : (side + 1) * cap, :], ret_halo.at[side],
            hb_s.at[side], hb_r.at[side],
            device_id={"nodes": left if side == 0 else right}, device_id_type=MESH,
        )

    def mix_home(d):
        return pltpu.make_async_remote_copy(
            gback.at[pl.ds(2 * cap + d * blk, blk), :], ret_mix.at[pl.ds(d * blk, blk), :],
            mb_s.at[d], mb_r.at[d],
            device_id={"nodes": lax.rem(me + n - d, n)}, device_id_type=MESH,
        )

    gk, gv = backward(chunks[1])
    gback[: 2 * cap, :width] = gk.astype(BF)
    gback[: 2 * cap, width:] = gv.astype(BF)
    home = [halo_home(0), halo_home(1)]
    for c in home:
        c.start()
    for c in chunks[2:]:
        gk, gv = backward(c)
        a = c[0] - rows
        gback[a : a + c[1], :width] = gk.astype(BF)
        gback[a : a + c[1], width:] = gv.astype(BF)
    each(n - 1, lambda d: mix_home(d + 1).start())
    gk, gv = backward(chunks[0])
    own_v[:, :width] = gk
    own_v[:, width:] = gv
    ret_mix[:blk, :] = gback[2 * cap : 2 * cap + blk, :]

    k_t = jnp.transpose(kv[:, :width])
    gq_t = jnp.concatenate(
        [
            mm(k_t[h * hd : (h + 1) * hd, :], ds_ref[:, h * rows : (h + 1) * rows], NN)
            for h in range(heads)
        ],
        axis=0,
    )
    gq_v[...] = jnp.transpose(gq_t * (hd ** -0.5))
    stores = [pltpu.make_async_copy(gq_v, gq_hbm, out_sem.at[0])]
    stores[-1].start()

    for d in range(1, mp):
        proj_copy(d).wait_recv()
        mine = mine + proj_in[d].astype(F32)
    out_v[...] = mine.astype(BF)
    stores.append(pltpu.make_async_copy(out_v, out_hbm, out_sem.at[1]))
    stores[-1].start()

    for c in home:
        c.wait_recv()
    acc = own_v[...] + mm(g_right, ret_halo[0], NN) + mm(g_left, ret_halo[1], NN)
    each(n - 1, lambda d: mix_home(d + 1).wait_recv())
    acc = acc + mm(onehot[...], ret_mix[...], TN)
    gk_v[...] = acc[:, :width]
    gv_v[...] = acc[:, width:]
    virt = jnp.sum(ret_mix[...].astype(F32).reshape(n, blk, 2 * width), axis=0)
    gvk_v[...] = virt[:vn, :width]
    gvv_v[...] = virt[:vn, width:]
    for i, (src, dst) in enumerate(
        ((gk_v, gk_hbm), (gv_v, gv_hbm), (gvk_v, gvk_hbm), (gvv_v, gvv_hbm))
    ):
        stores.append(pltpu.make_async_copy(src, dst, out_sem.at[2 + i]))
        stores[-1].start()

    for c in halo + home:
        c.wait_send()
    each(n - 1, lambda d: mix_copy(d + 1).wait_send())
    each(n - 1, lambda d: mix_home(d + 1).wait_send())
    for d in range(1, mp):
        cot_copy(d, mm_i).wait_send()
        proj_copy(d).wait_send()
    for c in stores:
        c.wait()


def hand_over(*refs):
    sem = refs[-1]
    copies = [pltpu.make_async_copy(refs[i], refs[6 + i], sem.at[i]) for i in range(6)]
    for c in copies:
        c.start()
    for c in copies:
        c.wait()


def solution(mesh):
    n, mp = mesh.shape["nodes"], mesh.shape["mp"]
    heads = HEADS // mp

    def step(q, k, v, w, cot, vk, vv, hrows, live, erows, lmask, emask):
        rows, width = q.shape
        cap, slots, vn = hrows.shape[2], erows.shape[2], vk.shape[0]
        blk = -(-(vn + slots) // 16) * 16
        total = rows + 2 * cap + n * blk
        hbm = pl.BlockSpec(memory_space=pltpu.HBM)
        anywhere = pl.BlockSpec(memory_space=pl.ANY)
        erows = jnp.swapaxes(erows, 1, 2)
        smalls = [pltpu.SMEM(x.shape, jnp.int32) for x in (live, erows, lmask, emask)]
        dma = pltpu.SemaphoreType.DMA
        flops = 2 * total * rows * width * 5
        operands = [
            pltpu.with_memory_space_constraint(x, pltpu.HBM)
            for x in (live, erows, lmask, emask, q, k, v, w, cot, vk, vv, hrows)
        ]
        results = pl.pallas_call(
            functools.partial(kernel, n, mp, heads),
            out_shape=(
                jax.ShapeDtypeStruct((rows, width), BF),
                jax.ShapeDtypeStruct((rows, width), F32),
                jax.ShapeDtypeStruct((rows, width), F32),
                jax.ShapeDtypeStruct((rows, width), F32),
                jax.ShapeDtypeStruct((vn, width), F32),
                jax.ShapeDtypeStruct((vn, width), F32),
            ),
            in_specs=[hbm] * 12,
            out_specs=(anywhere,) * 6,
            scratch_shapes=smalls + [
                pltpu.VMEM((rows, width), BF),
                pltpu.VMEM(w.shape, BF),
                pltpu.VMEM((vn, width), BF),
                pltpu.VMEM((vn, width), BF),
                pltpu.VMEM(hrows.shape, jnp.int32),
                pltpu.VMEM((total, 2 * width), BF),
                pltpu.VMEM((mp, rows, width), BF),
                pltpu.VMEM((total, width), BF),
                pltpu.VMEM((n * blk, rows), BF),
                pltpu.VMEM((n * blk, 2 * width), BF),
                pltpu.VMEM((2, cap, 2 * width), BF),
                pltpu.VMEM((total, heads * rows), F32),
                pltpu.VMEM((total, heads * rows), BF),
                pltpu.VMEM((total, heads * rows), BF),
                pltpu.VMEM((2 * cap + n * blk, 2 * width), BF),
                pltpu.VMEM((2, cap, 2 * width), BF),
                pltpu.VMEM((n * blk, 2 * width), BF),
                pltpu.VMEM((mp, rows, width), BF),
                pltpu.VMEM((mp, rows, width), BF),
                pltpu.VMEM((rows, 2 * width), F32),
                pltpu.VMEM((rows, width), BF),
                pltpu.VMEM((rows, width), F32),
                pltpu.VMEM((rows, width), F32),
                pltpu.VMEM((rows, width), F32),
                pltpu.VMEM((vn, width), F32),
                pltpu.VMEM((vn, width), F32),
                dma((12,)), dma((6,)),
                dma((2,)), dma((2,)), dma((n,)), dma((n,)),
                dma((mp,)), dma((mp,)), dma((mp,)), dma((mp,)),
                dma((2,)), dma((2,)), dma((n,)), dma((n,)),
            ],
            compiler_params=pltpu.CompilerParams(
                collective_id=0, has_side_effects=True, vmem_limit_bytes=62 << 20
            ),
            cost_estimate=pl.CostEstimate(
                flops=flops, transcendentals=total * rows * heads, bytes_accessed=2 << 20
            ),
        )(*operands)
        return pl.pallas_call(
            hand_over,
            out_shape=tuple(jax.ShapeDtypeStruct(x.shape, x.dtype) for x in results),
            in_specs=[anywhere] * 6,
            out_specs=(hbm,) * 6,
            scratch_shapes=[dma((6,))],
        )(*results)

    node = P("nodes", "mp")
    return jax.shard_map(
        step,
        mesh=mesh,
        in_specs=(
            node, node, node, P("mp", None), node, node, node,
            P("nodes", None, None), P("nodes", None), P("nodes", None, None),
            P("nodes", None), P("nodes", None),
        ),
        out_specs=(node,) * 6,
        check_vma=False,
    )
```

```python
import functools

import jax
import jax.numpy as jnp
from jax import lax
from jax.experimental import pallas as pl
from jax.experimental.pallas import tpu as pltpu
from jax.sharding import PartitionSpec as P

HEADS = 8
MESH = pl.DeviceIdType.MESH
BF = jnp.bfloat16
F32 = jnp.float32
MASKED = -1e30

NN = (((1,), (0,)), ((), ()))
NT = (((1,), (1,)), ((), ()))
TN = (((0,), (0,)), ((), ()))


def mm(a, b, dims):
    return lax.dot_general(a, b, dims, preferred_element_type=F32)


def iota(shape, axis):
    return lax.broadcasted_iota(jnp.int32, shape, axis)


def each(count, step):
    if count <= 8:
        for d in range(count):
            step(d)
    else:
        pl.loop(0, count)(step)


def kernel(
    n, mp, heads,
    live_hbm, erows_hbm, lmask_hbm, emask_hbm,
    q_hbm, k_hbm, v_hbm, w_hbm, cot_hbm, vk_hbm, vv_hbm, hrows_hbm,
    out_hbm, gq_hbm, gk_hbm, gv_hbm, gvk_hbm, gvv_hbm,
    live, erows, lmask, emask, q_v, w_v, vk_v, vv_v, hrows, kv, cot, bias, onehot, mix_send, halo_send,
    e_ref, pb_ref, ds_ref, gback, ret_halo, ret_mix, proj, proj_in, own_v,
    out_v, gq_v, gk_v, gv_v, gvk_v, gvv_v,
    in_sem, out_sem, halo_s, halo_r, mix_s, mix_r, cot_s, cot_r, proj_s, proj_r,
    hb_s, hb_r, mb_s, mb_r,
):
    me = lax.axis_index("nodes")
    mm_i = lax.axis_index("mp")
    rows, width = q_v.shape
    tiles = lmask.shape[0]
    tile = rows // tiles
    cap = hrows.shape[2]
    slots = erows.shape[1]
    vn = vk_v.shape[0]
    blk = ret_mix.shape[0] // n
    hd = width // heads
    cols = heads * rows
    left, right = lax.rem(me + n - 1, n), lax.rem(me + 1, n)
    mix0 = rows + 2 * cap
    total = mix0 + n * blk

    barrier = pltpu.get_barrier_semaphore()

    def hello(d):
        pl.semaphore_signal(
            barrier, inc=1, device_id={"nodes": lax.rem(me + d + 1, n)}, device_id_type=MESH
        )

    each(n - 1, hello)
    for d in range(1, mp):
        pl.semaphore_signal(
            barrier, inc=1, device_id={"mp": lax.rem(mm_i + d, mp)}, device_id_type=MESH
        )

    small = [
        pltpu.make_async_copy(src, dst, in_sem.at[8 + i])
        for i, (src, dst) in enumerate(
            ((erows_hbm, erows), (live_hbm, live), (lmask_hbm, lmask), (emask_hbm, emask))
        )
    ]
    for c in small:
        c.start()
    loads = [
        pltpu.make_async_copy(k_hbm, kv.at[:rows, :width], in_sem.at[0]),
        pltpu.make_async_copy(v_hbm, kv.at[:rows, width:], in_sem.at[1]),
        pltpu.make_async_copy(hrows_hbm, hrows, in_sem.at[2]),
        pltpu.make_async_copy(vk_hbm, vk_v, in_sem.at[3]),
        pltpu.make_async_copy(vv_hbm, vv_v, in_sem.at[4]),
        pltpu.make_async_copy(cot_hbm, cot.at[mm_i], in_sem.at[5]),
        pltpu.make_async_copy(q_hbm, q_v, in_sem.at[6]),
        pltpu.make_async_copy(w_hbm, w_v, in_sem.at[7]),
    ]
    for c in loads:
        c.start()

    row_b, lane_b = iota((blk, rows), 0), iota((blk, rows), 1)

    def fill(d):
        peer = lax.rem(me + d, n)
        target = jnp.full((blk, rows), -1, jnp.int32)
        for s in range(slots):
            target = jnp.where(row_b == vn + s, erows[0, s, peer], target)
        onehot[pl.ds(d * blk, blk), :] = jnp.where(lane_b == target, 1.0, 0.0).astype(BF)

    small[0].wait()
    each(n, fill)

    for c in loads[:5]:
        c.wait()
    own = kv[:rows, :]
    g_right = jnp.where(iota((rows, cap), 0) == hrows[0, 0:1, :], 1.0, 0.0).astype(BF)
    g_left = jnp.where(iota((rows, cap), 0) == hrows[0, 1:2, :], 1.0, 0.0).astype(BF)
    halo_send[0] = mm(g_right, own, TN).astype(BF)
    halo_send[1] = mm(g_left, own, TN).astype(BF)
    virt = jnp.concatenate([vk_v[...].astype(F32), vv_v[...].astype(F32)], axis=1)
    virt = jnp.concatenate([virt, jnp.zeros((blk - vn, 2 * width), F32)], axis=0)
    taken = mm(onehot[...], own, NN).reshape(n, blk, 2 * width) + virt[None]
    taken = taken.astype(BF)
    mix_send[...] = taken.reshape(n * blk, 2 * width)
    kv[mix0 : mix0 + blk, :] = taken[0]
    loads[5].wait()

    pl.semaphore_wait(barrier, n - 1 + mp - 1)

    def halo_copy(side):
        start = rows + side * cap
        return pltpu.make_async_remote_copy(
            halo_send.at[side], kv.at[start : start + cap, :], halo_s.at[side], halo_r.at[side],
            device_id={"nodes": right if side == 0 else left}, device_id_type=MESH,
        )

    def mix_copy(d):
        return pltpu.make_async_remote_copy(
            mix_send.at[pl.ds(d * blk, blk), :], kv.at[pl.ds(mix0 + d * blk, blk), :],
            mix_s.at[d], mix_r.at[d],
            device_id={"nodes": lax.rem(me + d, n)}, device_id_type=MESH,
        )

    def cot_copy(d, slot):
        return pltpu.make_async_remote_copy(
            cot.at[slot], cot.at[slot], cot_s.at[d], cot_r.at[d],
            device_id={"mp": lax.rem(mm_i + d, mp)}, device_id_type=MESH,
        )

    halo = [halo_copy(0), halo_copy(1)]
    for c in halo:
        c.start()
    each(n - 1, lambda d: mix_copy(d + 1).start())
    for d in range(1, mp):
        cot_copy(d, mm_i).start()

    for c in small[1:]:
        c.wait()

    lane = iota((1, width), 1)

    def per_tile(values):
        result = jnp.zeros(values[0].shape, F32)
        for t in range(tiles):
            result = jnp.where(lane == t, values[t], result)
        return result.astype(BF)

    def flag(x):
        return jnp.where(x > 0, 0.0, MASKED)

    for u in range(tiles):
        bias[u * tile : (u + 1) * tile, :] = per_tile(
            [jnp.full((tile, width), flag(lmask[t, u]), F32) for t in range(tiles)]
        )
    row_c = iota((cap, width), 0)
    for side in range(2):
        start = rows + side * cap
        bias[start : start + cap, :] = per_tile(
            [
                jnp.where(row_c < live[0, side], flag(lmask[t, tiles + side]), MASKED)
                for t in range(tiles)
            ]
        )
    row_m = iota((blk, width), 0)

    def mix_mask(d):
        source = lax.rem(me + n - d, n)
        values = []
        for t in range(tiles):
            inner = jnp.where(row_m < vn + slots, flag(emask[t, source]), MASKED)
            values.append(jnp.where(row_m < vn, 0.0, inner))
        bias[pl.ds(mix0 + d * blk, blk), :] = per_tile(values)

    each(n, mix_mask)

    feature = iota((width, rows), 0)

    def blocks(x):
        parts = []
        for h in range(heads):
            mine = (feature >= h * hd) & (feature < (h + 1) * hd)
            parts.append(jnp.where(mine, x, 0.0))
        return jnp.concatenate(parts, axis=1).astype(BF)

    loads[6].wait()
    q_t = jnp.transpose(q_v[...].astype(F32)) * (hd ** -0.5)
    q_blocks = blocks(q_t)
    col = iota((width, cols), 1)
    for h in range(1, heads):
        col = jnp.where(iota((width, cols), 1) >= h * rows, iota((width, cols), 1) - h * rows, col)
    tile_of = jnp.zeros((width, cols), jnp.int32)
    for t in range(1, tiles):
        tile_of = jnp.where(col >= t * tile, t, tile_of)
    in_tile = jnp.where(iota((width, cols), 0) == tile_of, 1.0, 0.0).astype(BF)
    q_aug = jnp.concatenate([q_blocks, in_tile], axis=0)

    chunks = [(0, rows), (rows, 2 * cap)]
    step_rows = min(n * blk, 256)
    chunks += [(mix0 + i, step_rows) for i in range(0, n * blk, step_rows)]

    def score(c):
        a, size = c
        keys = jnp.concatenate([kv[a : a + size, :width], bias[a : a + size, :]], axis=1)
        s = mm(keys, q_aug, NN)
        e_ref[a : a + size, :] = s
        return jnp.max(s, axis=0, keepdims=True)

    top = score(chunks[0])

    loads[7].wait()
    for d in range(1, mp):
        cot_copy(d, lax.rem(mm_i + mp - d, mp)).wait_recv()
    g_t = mm(w_v[...], jnp.concatenate([cot[i] for i in range(mp)], axis=1), NT)
    g_t = g_t.astype(BF).astype(F32)
    g_blocks = blocks(g_t)

    for c in halo:
        c.wait_recv()
    top = jnp.maximum(top, score(chunks[1]))
    each(n - 1, lambda d: mix_copy(d + 1).wait_recv())
    for c in chunks[2:]:
        top = jnp.maximum(top, score(c))

    norm = jnp.zeros((1, cols), F32)
    for a, size in chunks:
        e = jnp.exp(e_ref[a : a + size, :] - top)
        e_ref[a : a + size, :] = e
        norm = norm + jnp.sum(e, axis=0, keepdims=True)
    inv = 1.0 / norm
    for a, size in chunks:
        p = e_ref[a : a + size, :] * inv
        e_ref[a : a + size, :] = p
        pb_ref[a : a + size, :] = p.astype(BF)

    v_t = jnp.transpose(kv[:, width:])
    attn_t = jnp.concatenate(
        [
            mm(v_t[h * hd : (h + 1) * hd, :], pb_ref[:, h * rows : (h + 1) * rows], NN)
            for h in range(heads)
        ],
        axis=0,
    )
    attn_t = attn_t.astype(BF).astype(F32)
    prod = g_t * attn_t
    delta = jnp.concatenate(
        [jnp.sum(prod[h * hd : (h + 1) * hd, :], axis=0, keepdims=True) for h in range(heads)],
        axis=1,
    )
    attn = jnp.transpose(attn_t).astype(BF)

    def proj_copy(d):
        peer = lax.rem(mm_i + d, mp)
        return pltpu.make_async_remote_copy(
            proj.at[peer], proj_in.at[d], proj_s.at[d], proj_r.at[d],
            device_id={"mp": peer}, device_id_type=MESH,
        )

    full = mm(attn, w_v[...], NN)
    for i in range(mp):
        proj[i] = full[:, i * width : (i + 1) * width].astype(BF)
    for d in range(1, mp):
        proj_copy(d).start()
    mine = mm(attn, w_v[:, pl.ds(pl.multiple_of(mm_i * width, width), width)], NN)

    def backward(c):
        a, size = c
        dp = mm(kv[a : a + size, width:], g_blocks, NN)
        ds = (e_ref[a : a + size, :] * (dp - delta)).astype(BF)
        ds_ref[a : a + size, :] = ds
        gk = mm(ds, q_blocks, NT)
        gv = mm(pb_ref[a : a + size, :], g_blocks, NT)
        return gk, gv

    def halo_home(side):
        return pltpu.make_async_remote_copy(
            gback.at[side * cap : (side + 1) * cap, :], ret_halo.at[side],
            hb_s.at[side], hb_r.at[side],
            device_id={"nodes": left if side == 0 else right}, device_id_type=MESH,
        )

    def mix_home(d):
        return pltpu.make_async_remote_copy(
            gback.at[pl.ds(2 * cap + d * blk, blk), :], ret_mix.at[pl.ds(d * blk, blk), :],
            mb_s.at[d], mb_r.at[d],
            device_id={"nodes": lax.rem(me + n - d, n)}, device_id_type=MESH,
        )

    gk, gv = backward(chunks[1])
    gback[: 2 * cap, :width] = gk.astype(BF)
    gback[: 2 * cap, width:] = gv.astype(BF)
    home = [halo_home(0), halo_home(1)]
    for c in home:
        c.start()
    for c in chunks[2:]:
        gk, gv = backward(c)
        a = c[0] - rows
        gback[a : a + c[1], :width] = gk.astype(BF)
        gback[a : a + c[1], width:] = gv.astype(BF)
    each(n - 1, lambda d: mix_home(d + 1).start())
    gk, gv = backward(chunks[0])
    own_v[:, :width] = gk
    own_v[:, width:] = gv
    ret_mix[:blk, :] = gback[2 * cap : 2 * cap + blk, :]

    k_t = jnp.transpose(kv[:, :width])
    gq_t = jnp.concatenate(
        [
            mm(k_t[h * hd : (h + 1) * hd, :], ds_ref[:, h * rows : (h + 1) * rows], NN)
            for h in range(heads)
        ],
        axis=0,
    )
    gq_v[...] = jnp.transpose(gq_t * (hd ** -0.5))
    stores = [pltpu.make_async_copy(gq_v, gq_hbm, out_sem.at[0])]
    stores[-1].start()

    for d in range(1, mp):
        proj_copy(d).wait_recv()
        mine = mine + proj_in[d].astype(F32)
    out_v[...] = mine.astype(BF)
    stores.append(pltpu.make_async_copy(out_v, out_hbm, out_sem.at[1]))
    stores[-1].start()

    for c in home:
        c.wait_recv()
    acc = own_v[...] + mm(g_right, ret_halo[0], NN) + mm(g_left, ret_halo[1], NN)
    each(n - 1, lambda d: mix_home(d + 1).wait_recv())
    acc = acc + mm(onehot[...], ret_mix[...], TN)
    gk_v[...] = acc[:, :width]
    gv_v[...] = acc[:, width:]
    virt = jnp.sum(ret_mix[...].astype(F32).reshape(n, blk, 2 * width), axis=0)
    gvk_v[...] = virt[:vn, :width]
    gvv_v[...] = virt[:vn, width:]
    for i, (src, dst) in enumerate(
        ((gk_v, gk_hbm), (gv_v, gv_hbm), (gvk_v, gvk_hbm), (gvv_v, gvv_hbm))
    ):
        stores.append(pltpu.make_async_copy(src, dst, out_sem.at[2 + i]))
        stores[-1].start()

    for c in halo + home:
        c.wait_send()
    each(n - 1, lambda d: mix_copy(d + 1).wait_send())
    each(n - 1, lambda d: mix_home(d + 1).wait_send())
    for d in range(1, mp):
        cot_copy(d, mm_i).wait_send()
        proj_copy(d).wait_send()
    for c in stores:
        c.wait()


def hand_over(*refs):
    sem = refs[-1]
    copies = [pltpu.make_async_copy(refs[i], refs[6 + i], sem.at[i]) for i in range(6)]
    for c in copies:
        c.start()
    for c in copies:
        c.wait()


def solution(mesh):
    n, mp = mesh.shape["nodes"], mesh.shape["mp"]
    heads = HEADS // mp

    def step(q, k, v, w, cot, vk, vv, hrows, live, erows, lmask, emask):
        rows, width = q.shape
        cap, slots, vn = hrows.shape[2], erows.shape[2], vk.shape[0]
        blk = -(-(vn + slots) // 16) * 16
        total = rows + 2 * cap + n * blk
        hbm = pl.BlockSpec(memory_space=pltpu.HBM)
        anywhere = pl.BlockSpec(memory_space=pl.ANY)
        erows = jnp.swapaxes(erows, 1, 2)
        smalls = [pltpu.SMEM(x.shape, jnp.int32) for x in (live, erows, lmask, emask)]
        dma = pltpu.SemaphoreType.DMA
        flops = 2 * total * rows * width * 5
        operands = [
            pltpu.with_memory_space_constraint(x, pltpu.HBM)
            for x in (live, erows, lmask, emask, q, k, v, w, cot, vk, vv, hrows)
        ]
        results = pl.pallas_call(
            functools.partial(kernel, n, mp, heads),
            out_shape=(
                jax.ShapeDtypeStruct((rows, width), BF),
                jax.ShapeDtypeStruct((rows, width), F32),
                jax.ShapeDtypeStruct((rows, width), F32),
                jax.ShapeDtypeStruct((rows, width), F32),
                jax.ShapeDtypeStruct((vn, width), F32),
                jax.ShapeDtypeStruct((vn, width), F32),
            ),
            in_specs=[hbm] * 12,
            out_specs=(anywhere,) * 6,
            scratch_shapes=smalls + [
                pltpu.VMEM((rows, width), BF),
                pltpu.VMEM(w.shape, BF),
                pltpu.VMEM((vn, width), BF),
                pltpu.VMEM((vn, width), BF),
                pltpu.VMEM(hrows.shape, jnp.int32),
                pltpu.VMEM((total, 2 * width), BF),
                pltpu.VMEM((mp, rows, width), BF),
                pltpu.VMEM((total, width), BF),
                pltpu.VMEM((n * blk, rows), BF),
                pltpu.VMEM((n * blk, 2 * width), BF),
                pltpu.VMEM((2, cap, 2 * width), BF),
                pltpu.VMEM((total, heads * rows), F32),
                pltpu.VMEM((total, heads * rows), BF),
                pltpu.VMEM((total, heads * rows), BF),
                pltpu.VMEM((2 * cap + n * blk, 2 * width), BF),
                pltpu.VMEM((2, cap, 2 * width), BF),
                pltpu.VMEM((n * blk, 2 * width), BF),
                pltpu.VMEM((mp, rows, width), BF),
                pltpu.VMEM((mp, rows, width), BF),
                pltpu.VMEM((rows, 2 * width), F32),
                pltpu.VMEM((rows, width), BF),
                pltpu.VMEM((rows, width), F32),
                pltpu.VMEM((rows, width), F32),
                pltpu.VMEM((rows, width), F32),
                pltpu.VMEM((vn, width), F32),
                pltpu.VMEM((vn, width), F32),
                dma((12,)), dma((6,)),
                dma((2,)), dma((2,)), dma((n,)), dma((n,)),
                dma((mp,)), dma((mp,)), dma((mp,)), dma((mp,)),
                dma((2,)), dma((2,)), dma((n,)), dma((n,)),
            ],
            compiler_params=pltpu.CompilerParams(
                collective_id=0, has_side_effects=True, vmem_limit_bytes=40 << 20
            ),
            cost_estimate=pl.CostEstimate(
                flops=flops, transcendentals=total * rows * heads, bytes_accessed=2 << 20
            ),
        )(*operands)
        return pl.pallas_call(
            hand_over,
            out_shape=tuple(jax.ShapeDtypeStruct(x.shape, x.dtype) for x in results),
            in_specs=[anywhere] * 6,
            out_specs=(hbm,) * 6,
            scratch_shapes=[dma((6,))],
            compiler_params=pltpu.CompilerParams(vmem_limit_bytes=4 << 20),
            cost_estimate=pl.CostEstimate(flops=0, transcendentals=0, bytes_accessed=1 << 20),
        )(*results)

    node = P("nodes", "mp")
    return jax.shard_map(
        step,
        mesh=mesh,
        in_specs=(
            node, node, node, P("mp", None), node, node, node,
            P("nodes", None, None), P("nodes", None), P("nodes", None, None),
            P("nodes", None), P("nodes", None),
        ),
        out_specs=(node,) * 6,
        check_vma=False,
    )
```

```python
import functools

import jax
import jax.numpy as jnp
from jax import lax
from jax.experimental import pallas as pl
from jax.experimental.pallas import tpu as pltpu
from jax.sharding import PartitionSpec as P

HEADS = 8
MESH = pl.DeviceIdType.MESH
BF = jnp.bfloat16
F32 = jnp.float32
MASKED = -1e30

NN = (((1,), (0,)), ((), ()))
NT = (((1,), (1,)), ((), ()))
TN = (((0,), (0,)), ((), ()))


def mm(a, b, dims):
    return lax.dot_general(a, b, dims, preferred_element_type=F32)


def iota(shape, axis):
    return lax.broadcasted_iota(jnp.int32, shape, axis)


def each(count, step):
    if count <= 8:
        for d in range(count):
            step(d)
    else:
        pl.loop(0, count)(step)


def kernel(
    n, mp, heads,
    live_hbm, erows_hbm, lmask_hbm, emask_hbm,
    q_hbm, k_hbm, v_hbm, w_hbm, cot_hbm, vk_hbm, vv_hbm, hrows_hbm,
    out_v, gq_v, gk_v, gv_v, gvk_v, gvv_v,
    live, erows, lmask, emask, q_v, w_v, vk_v, vv_v, hrows, kv, cot, bias, onehot, mix_send, halo_send,
    kvt, e_ref, pb_ref, ds_ref, gback, ret_halo, ret_mix, proj, proj_in, own_v,
    in_sem, halo_s, halo_r, mix_s, mix_r, cot_s, cot_r, proj_s, proj_r,
    hb_s, hb_r, mb_s, mb_r,
):
    me = lax.axis_index("nodes")
    mm_i = lax.axis_index("mp")
    rows, width = q_v.shape
    tiles = lmask.shape[0]
    tile = rows // tiles
    cap = hrows.shape[2]
    slots = erows.shape[1]
    vn = vk_v.shape[0]
    blk = ret_mix.shape[0] // n
    hd = width // heads
    cols = heads * rows
    left, right = lax.rem(me + n - 1, n), lax.rem(me + 1, n)
    mix0 = rows + 2 * cap
    total = mix0 + n * blk

    barrier = pltpu.get_barrier_semaphore()

    def hello(d):
        pl.semaphore_signal(
            barrier, inc=1, device_id={"nodes": lax.rem(me + d + 1, n)}, device_id_type=MESH
        )

    each(n - 1, hello)
    for d in range(1, mp):
        pl.semaphore_signal(
            barrier, inc=1, device_id={"mp": lax.rem(mm_i + d, mp)}, device_id_type=MESH
        )

    small = [
        pltpu.make_async_copy(src, dst, in_sem.at[8 + i])
        for i, (src, dst) in enumerate(
            ((erows_hbm, erows), (live_hbm, live), (lmask_hbm, lmask), (emask_hbm, emask))
        )
    ]
    for c in small:
        c.start()
    loads = [
        pltpu.make_async_copy(k_hbm, kv.at[:rows, :width], in_sem.at[0]),
        pltpu.make_async_copy(v_hbm, kv.at[:rows, width:], in_sem.at[1]),
        pltpu.make_async_copy(hrows_hbm, hrows, in_sem.at[2]),
        pltpu.make_async_copy(vk_hbm, vk_v, in_sem.at[3]),
        pltpu.make_async_copy(vv_hbm, vv_v, in_sem.at[4]),
        pltpu.make_async_copy(cot_hbm, cot.at[mm_i], in_sem.at[5]),
        pltpu.make_async_copy(q_hbm, q_v, in_sem.at[6]),
        pltpu.make_async_copy(w_hbm, w_v, in_sem.at[7]),
    ]
    for c in loads:
        c.start()

    row_b, lane_b = iota((blk, rows), 0), iota((blk, rows), 1)

    def fill(d):
        peer = lax.rem(me + d, n)
        target = jnp.full((blk, rows), -1, jnp.int32)
        for s in range(slots):
            target = jnp.where(row_b == vn + s, erows[0, s, peer], target)
        onehot[pl.ds(d * blk, blk), :] = jnp.where(lane_b == target, 1.0, 0.0).astype(BF)

    small[0].wait()
    each(n, fill)

    for c in loads[:3]:
        c.wait()
    own = kv[:rows, :]
    wanted = jnp.concatenate([hrows[0].astype(F32), jnp.zeros((6, cap), F32)], axis=0)
    wanted = jnp.transpose(wanted).astype(jnp.int32)
    wanted = jnp.concatenate([wanted[:, 0:1], wanted[:, 1:2]], axis=0)
    picks = jnp.where(iota((2 * cap, rows), 1) == wanted, 1.0, 0.0).astype(BF)
    halo_send[...] = mm(picks, own, NN).astype(BF).reshape(2, cap, 2 * width)

    pl.semaphore_wait(barrier, n - 1 + mp - 1)

    def halo_copy(side):
        start = rows + side * cap
        return pltpu.make_async_remote_copy(
            halo_send.at[side], kv.at[start : start + cap, :], halo_s.at[side], halo_r.at[side],
            device_id={"nodes": right if side == 0 else left}, device_id_type=MESH,
        )

    def mix_copy(d):
        return pltpu.make_async_remote_copy(
            mix_send.at[pl.ds(d * blk, blk), :], kv.at[pl.ds(mix0 + d * blk, blk), :],
            mix_s.at[d], mix_r.at[d],
            device_id={"nodes": lax.rem(me + d, n)}, device_id_type=MESH,
        )

    def cot_copy(d, slot):
        return pltpu.make_async_remote_copy(
            cot.at[slot], cot.at[slot], cot_s.at[d], cot_r.at[d],
            device_id={"mp": lax.rem(mm_i + d, mp)}, device_id_type=MESH,
        )

    halo = [halo_copy(0), halo_copy(1)]
    for c in halo:
        c.start()

    for c in loads[3:6]:
        c.wait()
    virt = jnp.concatenate([vk_v[...].astype(F32), vv_v[...].astype(F32)], axis=1)
    virt = jnp.concatenate([virt, jnp.zeros((blk - vn, 2 * width), F32)], axis=0)
    taken = mm(onehot[...], own, NN).reshape(n, blk, 2 * width) + virt[None]
    taken = taken.astype(BF)
    mix_send[...] = taken.reshape(n * blk, 2 * width)
    each(n - 1, lambda d: mix_copy(d + 1).start())
    for d in range(1, mp):
        cot_copy(d, mm_i).start()
    kv[mix0 : mix0 + blk, :] = taken[0]
    for c in small[1:]:
        c.wait()

    lane = iota((1, width), 1)

    def per_tile(values):
        result = jnp.zeros(values[0].shape, F32)
        for t in range(tiles):
            result = jnp.where(lane == t, values[t], result)
        return result.astype(BF)

    def flag(x):
        return jnp.where(x > 0, 0.0, MASKED)

    for u in range(tiles):
        bias[u * tile : (u + 1) * tile, :] = per_tile(
            [jnp.full((tile, width), flag(lmask[t, u]), F32) for t in range(tiles)]
        )
    row_c = iota((cap, width), 0)
    for side in range(2):
        start = rows + side * cap
        bias[start : start + cap, :] = per_tile(
            [
                jnp.where(row_c < live[0, side], flag(lmask[t, tiles + side]), MASKED)
                for t in range(tiles)
            ]
        )
    row_m = iota((blk, width), 0)

    def mix_mask(d):
        source = lax.rem(me + n - d, n)
        values = []
        for t in range(tiles):
            inner = jnp.where(row_m < vn + slots, flag(emask[t, source]), MASKED)
            values.append(jnp.where(row_m < vn, 0.0, inner))
        bias[pl.ds(mix0 + d * blk, blk), :] = per_tile(values)

    each(n, mix_mask)

    feature = iota((width, rows), 0)

    def blocks(x):
        parts = []
        for h in range(heads):
            mine = (feature >= h * hd) & (feature < (h + 1) * hd)
            parts.append(jnp.where(mine, x, 0.0))
        return jnp.concatenate(parts, axis=1).astype(BF)

    loads[6].wait()
    q_t = jnp.transpose(q_v[...].astype(F32)) * (hd ** -0.5)
    q_blocks = blocks(q_t)
    col = iota((width, cols), 1)
    for h in range(1, heads):
        col = jnp.where(iota((width, cols), 1) >= h * rows, iota((width, cols), 1) - h * rows, col)
    tile_of = jnp.zeros((width, cols), jnp.int32)
    for t in range(1, tiles):
        tile_of = jnp.where(col >= t * tile, t, tile_of)
    in_tile = jnp.where(iota((width, cols), 0) == tile_of, 1.0, 0.0).astype(BF)
    q_aug = jnp.concatenate([q_blocks, in_tile], axis=0)

    chunks = [(0, rows), (rows, 2 * cap)]
    step_rows = min(n * blk, 256)
    chunks += [(mix0 + i, step_rows) for i in range(0, n * blk, step_rows)]

    def score(c):
        a, size = c
        keys = jnp.concatenate([kv[a : a + size, :width], bias[a : a + size, :]], axis=1)
        s = mm(keys, q_aug, NN)
        top = jnp.max(s, axis=0, keepdims=True)
        e = jnp.exp(s - top)
        e_ref[a : a + size, :] = e
        kvt[:, a : a + size] = jnp.transpose(kv[a : a + size, :])
        return top, jnp.sum(e, axis=0, keepdims=True)

    stats = [score(chunks[0])]
    g_right = jnp.where(iota((rows, cap), 0) == hrows[0, 0:1, :], 1.0, 0.0).astype(BF)
    g_left = jnp.where(iota((rows, cap), 0) == hrows[0, 1:2, :], 1.0, 0.0).astype(BF)
    for c in halo:
        c.wait_recv()
    stats.append(score(chunks[1]))
    each(n - 1, lambda d: mix_copy(d + 1).wait_recv())
    for c in chunks[2:]:
        stats.append(score(c))

    top = functools.reduce(jnp.maximum, [t for t, _ in stats])
    factor = [jnp.exp(t - top) for t, _ in stats]
    norm = sum(f * z for f, (_, z) in zip(factor, stats))
    inv = 1.0 / norm
    factor = {c: f * inv for c, f in zip(chunks, factor)}
    for a, size in chunks:
        pb_ref[a : a + size, :] = (e_ref[a : a + size, :] * factor[(a, size)]).astype(BF)

    attn_t = jnp.concatenate(
        [
            mm(
                kvt[width + h * hd : width + (h + 1) * hd, :],
                pb_ref[:, h * rows : (h + 1) * rows],
                NN,
            )
            for h in range(heads)
        ],
        axis=0,
    )
    attn_t = attn_t.astype(BF).astype(F32)
    loads[7].wait()
    attn = jnp.transpose(attn_t).astype(BF)

    def proj_copy(d):
        peer = lax.rem(mm_i + d, mp)
        return pltpu.make_async_remote_copy(
            proj.at[peer], proj_in.at[d], proj_s.at[d], proj_r.at[d],
            device_id={"mp": peer}, device_id_type=MESH,
        )

    full = mm(attn, w_v[...], NN)
    for i in range(mp):
        proj[i] = full[:, i * width : (i + 1) * width].astype(BF)
    for d in range(1, mp):
        proj_copy(d).start()

    for d in range(1, mp):
        cot_copy(d, lax.rem(mm_i + mp - d, mp)).wait_recv()
    g_t = mm(w_v[...], jnp.concatenate([cot[i] for i in range(mp)], axis=1), NT)
    g_t = g_t.astype(BF).astype(F32)
    g_blocks = blocks(g_t)
    prod = g_t * attn_t
    delta = jnp.concatenate(
        [jnp.sum(prod[h * hd : (h + 1) * hd, :], axis=0, keepdims=True) for h in range(heads)],
        axis=1,
    )

    def backward(c):
        a, size = c
        dp = mm(kv[a : a + size, width:], g_blocks, NN)
        ds = (e_ref[a : a + size, :] * factor[c] * (dp - delta)).astype(BF)
        ds_ref[a : a + size, :] = ds
        gk = mm(ds, q_blocks, NT)
        gv = mm(pb_ref[a : a + size, :], g_blocks, NT)
        return gk, gv

    def halo_home(side):
        return pltpu.make_async_remote_copy(
            gback.at[side * cap : (side + 1) * cap, :], ret_halo.at[side],
            hb_s.at[side], hb_r.at[side],
            device_id={"nodes": left if side == 0 else right}, device_id_type=MESH,
        )

    def mix_home(d):
        return pltpu.make_async_remote_copy(
            gback.at[pl.ds(2 * cap + d * blk, blk), :], ret_mix.at[pl.ds(d * blk, blk), :],
            mb_s.at[d], mb_r.at[d],
            device_id={"nodes": lax.rem(me + n - d, n)}, device_id_type=MESH,
        )

    gk, gv = backward(chunks[1])
    gback[: 2 * cap, :width] = gk.astype(BF)
    gback[: 2 * cap, width:] = gv.astype(BF)
    home = [halo_home(0), halo_home(1)]
    for c in home:
        c.start()
    for c in chunks[2:]:
        gk, gv = backward(c)
        a = c[0] - rows
        gback[a : a + c[1], :width] = gk.astype(BF)
        gback[a : a + c[1], width:] = gv.astype(BF)
    each(n - 1, lambda d: mix_home(d + 1).start())
    gk, gv = backward(chunks[0])
    own_v[:, :width] = gk
    own_v[:, width:] = gv
    ret_mix[:blk, :] = gback[2 * cap : 2 * cap + blk, :]

    gq_t = jnp.concatenate(
        [
            mm(kvt[h * hd : (h + 1) * hd, :], ds_ref[:, h * rows : (h + 1) * rows], NN)
            for h in range(heads)
        ],
        axis=0,
    )
    gq_v[...] = jnp.transpose(gq_t * (hd ** -0.5))

    mine = mm(attn, w_v[:, pl.ds(pl.multiple_of(mm_i * width, width), width)], NN)
    for d in range(1, mp):
        proj_copy(d).wait_recv()
        mine = mine + proj_in[d].astype(F32)
    out_v[...] = mine.astype(BF)

    for c in home:
        c.wait_recv()
    acc = own_v[...] + mm(g_right, ret_halo[0], NN) + mm(g_left, ret_halo[1], NN)
    each(n - 1, lambda d: mix_home(d + 1).wait_recv())
    acc = acc + mm(onehot[...], ret_mix[...], TN)
    gk_v[...] = acc[:, :width]
    gv_v[...] = acc[:, width:]
    virt = jnp.sum(ret_mix[...].astype(F32).reshape(n, blk, 2 * width), axis=0)
    gvk_v[...] = virt[:vn, :width]
    gvv_v[...] = virt[:vn, width:]
    for c in halo + home:
        c.wait_send()
    each(n - 1, lambda d: mix_copy(d + 1).wait_send())
    each(n - 1, lambda d: mix_home(d + 1).wait_send())
    for d in range(1, mp):
        cot_copy(d, mm_i).wait_send()
        proj_copy(d).wait_send()


def hand_over(*refs):
    sem = refs[-1]
    copies = [pltpu.make_async_copy(refs[i], refs[6 + i], sem.at[i]) for i in range(6)]
    for c in copies:
        c.start()
    for c in copies:
        c.wait()


def solution(mesh):
    n, mp = mesh.shape["nodes"], mesh.shape["mp"]
    heads = HEADS // mp

    def step(q, k, v, w, cot, vk, vv, hrows, live, erows, lmask, emask):
        rows, width = q.shape
        cap, slots, vn = hrows.shape[2], erows.shape[2], vk.shape[0]
        blk = -(-(vn + slots) // 16) * 16
        total = rows + 2 * cap + n * blk
        hbm = pl.BlockSpec(memory_space=pltpu.HBM)
        anywhere = pl.BlockSpec(memory_space=pl.ANY)
        erows = jnp.swapaxes(erows, 1, 2)
        smalls = [pltpu.SMEM(x.shape, jnp.int32) for x in (live, erows, lmask, emask)]
        dma = pltpu.SemaphoreType.DMA
        flops = 2 * total * rows * width * 5
        operands = [
            pltpu.with_memory_space_constraint(x, pltpu.HBM)
            for x in (live, erows, lmask, emask, q, k, v, w, cot, vk, vv, hrows)
        ]
        results = pl.pallas_call(
            functools.partial(kernel, n, mp, heads),
            out_shape=(
                jax.ShapeDtypeStruct((rows, width), BF),
                jax.ShapeDtypeStruct((rows, width), F32),
                jax.ShapeDtypeStruct((rows, width), F32),
                jax.ShapeDtypeStruct((rows, width), F32),
                jax.ShapeDtypeStruct((vn, width), F32),
                jax.ShapeDtypeStruct((vn, width), F32),
            ),
            in_specs=[hbm] * 12,
            out_specs=(pl.BlockSpec(memory_space=pltpu.VMEM),) * 6,
            scratch_shapes=smalls + [
                pltpu.VMEM((rows, width), BF),
                pltpu.VMEM(w.shape, BF),
                pltpu.VMEM((vn, width), BF),
                pltpu.VMEM((vn, width), BF),
                pltpu.VMEM(hrows.shape, jnp.int32),
                pltpu.VMEM((total, 2 * width), BF),
                pltpu.VMEM((mp, rows, width), BF),
                pltpu.VMEM((total, width), BF),
                pltpu.VMEM((n * blk, rows), BF),
                pltpu.VMEM((n * blk, 2 * width), BF),
                pltpu.VMEM((2, cap, 2 * width), BF),
                pltpu.VMEM((2 * width, total), BF),
                pltpu.VMEM((total, heads * rows), F32),
                pltpu.VMEM((total, heads * rows), BF),
                pltpu.VMEM((total, heads * rows), BF),
                pltpu.VMEM((2 * cap + n * blk, 2 * width), BF),
                pltpu.VMEM((2, cap, 2 * width), BF),
                pltpu.VMEM((n * blk, 2 * width), BF),
                pltpu.VMEM((mp, rows, width), BF),
                pltpu.VMEM((mp, rows, width), BF),
                pltpu.VMEM((rows, 2 * width), F32),
                dma((12,)),
                dma((2,)), dma((2,)), dma((n,)), dma((n,)),
                dma((mp,)), dma((mp,)), dma((mp,)), dma((mp,)),
                dma((2,)), dma((2,)), dma((n,)), dma((n,)),
            ],
            compiler_params=pltpu.CompilerParams(
                collective_id=0, has_side_effects=True, vmem_limit_bytes=40 << 20
            ),
            cost_estimate=pl.CostEstimate(
                flops=flops, transcendentals=total * rows * heads, bytes_accessed=2 << 20
            ),
        )(*operands)
        return pl.pallas_call(
            hand_over,
            out_shape=tuple(jax.ShapeDtypeStruct(x.shape, x.dtype) for x in results),
            in_specs=[anywhere] * 6,
            out_specs=(hbm,) * 6,
            scratch_shapes=[dma((6,))],
            compiler_params=pltpu.CompilerParams(vmem_limit_bytes=4 << 20),
            cost_estimate=pl.CostEstimate(flops=0, transcendentals=0, bytes_accessed=1 << 20),
        )(*results)

    node = P("nodes", "mp")
    return jax.shard_map(
        step,
        mesh=mesh,
        in_specs=(
            node, node, node, P("mp", None), node, node, node,
            P("nodes", None, None), P("nodes", None), P("nodes", None, None),
            P("nodes", None), P("nodes", None),
        ),
        out_specs=(node,) * 6,
        check_vma=False,
    )
```

```python
import functools

import jax
import jax.numpy as jnp
from jax import lax
from jax.experimental import pallas as pl
from jax.experimental.pallas import tpu as pltpu
from jax.sharding import PartitionSpec as P

HEADS = 8
MESH = pl.DeviceIdType.MESH
BF = jnp.bfloat16
F32 = jnp.float32
MASKED = -1e30

NN = (((1,), (0,)), ((), ()))
NT = (((1,), (1,)), ((), ()))
TN = (((0,), (0,)), ((), ()))


def mm(a, b, dims):
    return lax.dot_general(a, b, dims, preferred_element_type=F32)


def iota(shape, axis):
    return lax.broadcasted_iota(jnp.int32, shape, axis)


def each(count, step):
    if count <= 8:
        for d in range(count):
            step(d)
    else:
        pl.loop(0, count)(step)


def kernel(
    n, mp, heads,
    live_hbm, erows_hbm, lmask_hbm, emask_hbm,
    q_hbm, k_hbm, v_hbm, w_hbm, cot_hbm, vk_hbm, vv_hbm, hrows_hbm,
    out_v, gq_v, gk_v, gv_v, gvk_v, gvv_v,
    live, erows, lmask, emask, q_v, w_v, vk_v, vv_v, hrows, kv, cot, bias, onehot, mix_send, halo_send,
    kvt, e_ref, pb_ref, ds_ref, gback, ret_halo, ret_mix, proj, proj_in, own_v,
    in_sem, halo_s, halo_r, mix_s, mix_r, cot_s, cot_r, proj_s, proj_r,
    hb_s, hb_r, mb_s, mb_r,
):
    me = lax.axis_index("nodes")
    mm_i = lax.axis_index("mp")
    rows, width = q_v.shape
    tiles = lmask.shape[0]
    tile = rows // tiles
    cap = hrows.shape[2]
    slots = erows.shape[1]
    vn = vk_v.shape[0]
    blk = ret_mix.shape[0] // n
    hd = width // heads
    cols = heads * rows
    left, right = lax.rem(me + n - 1, n), lax.rem(me + 1, n)
    mix0 = rows + 2 * cap
    total = mix0 + n * blk

    barrier = pltpu.get_barrier_semaphore()

    def hello(d):
        pl.semaphore_signal(
            barrier, inc=1, device_id={"nodes": lax.rem(me + d + 1, n)}, device_id_type=MESH
        )

    each(n - 1, hello)
    for d in range(1, mp):
        pl.semaphore_signal(
            barrier, inc=1, device_id={"mp": lax.rem(mm_i + d, mp)}, device_id_type=MESH
        )

    small = [
        pltpu.make_async_copy(src, dst, in_sem.at[8 + i])
        for i, (src, dst) in enumerate(
            ((erows_hbm, erows), (live_hbm, live), (lmask_hbm, lmask), (emask_hbm, emask))
        )
    ]
    for c in small:
        c.start()
    loads = [
        pltpu.make_async_copy(k_hbm, kv.at[:rows, :width], in_sem.at[0]),
        pltpu.make_async_copy(v_hbm, kv.at[:rows, width:], in_sem.at[1]),
        pltpu.make_async_copy(hrows_hbm, hrows, in_sem.at[2]),
        pltpu.make_async_copy(vk_hbm, vk_v, in_sem.at[3]),
        pltpu.make_async_copy(vv_hbm, vv_v, in_sem.at[4]),
        pltpu.make_async_copy(cot_hbm, cot.at[mm_i], in_sem.at[5]),
        pltpu.make_async_copy(q_hbm, q_v, in_sem.at[6]),
        pltpu.make_async_copy(w_hbm, w_v, in_sem.at[7]),
    ]
    for c in loads:
        c.start()

    row_b, lane_b = iota((blk, rows), 0), iota((blk, rows), 1)

    def fill(d):
        peer = lax.rem(me + d, n)
        target = jnp.full((blk, rows), -1, jnp.int32)
        for s in range(slots):
            target = jnp.where(row_b == vn + s, erows[0, s, peer], target)
        onehot[pl.ds(d * blk, blk), :] = jnp.where(lane_b == target, 1.0, 0.0).astype(BF)

    small[0].wait()
    each(n, fill)

    for c in loads[:3]:
        c.wait()
    own = kv[:rows, :]
    wanted = jnp.concatenate([hrows[0].astype(F32), jnp.zeros((6, cap), F32)], axis=0)
    wanted = jnp.transpose(wanted).astype(jnp.int32)
    wanted = jnp.concatenate([wanted[:, 0:1], wanted[:, 1:2]], axis=0)
    picks = jnp.where(iota((2 * cap, rows), 1) == wanted, 1.0, 0.0).astype(BF)
    halo_send[...] = mm(picks, own, NN).astype(BF).reshape(2, cap, 2 * width)

    pl.semaphore_wait(barrier, n - 1 + mp - 1)

    def halo_copy(side):
        start = rows + side * cap
        return pltpu.make_async_remote_copy(
            halo_send.at[side], kv.at[start : start + cap, :], halo_s.at[side], halo_r.at[side],
            device_id={"nodes": right if side == 0 else left}, device_id_type=MESH,
        )

    def mix_copy(d):
        return pltpu.make_async_remote_copy(
            mix_send.at[pl.ds(d * blk, blk), :], kv.at[pl.ds(mix0 + d * blk, blk), :],
            mix_s.at[d], mix_r.at[d],
            device_id={"nodes": lax.rem(me + d, n)}, device_id_type=MESH,
        )

    def cot_copy(d, slot):
        return pltpu.make_async_remote_copy(
            cot.at[slot], cot.at[slot], cot_s.at[d], cot_r.at[d],
            device_id={"mp": lax.rem(mm_i + d, mp)}, device_id_type=MESH,
        )

    halo = [halo_copy(0), halo_copy(1)]
    for c in halo:
        c.start()

    loads[5].wait()
    for d in range(1, mp):
        cot_copy(d, mm_i).start()

    for c in loads[3:5]:
        c.wait()
    virt = jnp.concatenate([vk_v[...].astype(F32), vv_v[...].astype(F32)], axis=1)
    virt = jnp.concatenate([virt, jnp.zeros((blk - vn, 2 * width), F32)], axis=0)
    taken = mm(onehot[...], own, NN).reshape(n, blk, 2 * width) + virt[None]
    taken = taken.astype(BF)
    mix_send[...] = taken.reshape(n * blk, 2 * width)
    each(n - 1, lambda d: mix_copy(d + 1).start())
    kv[mix0 : mix0 + blk, :] = taken[0]
    for c in small[1:]:
        c.wait()

    lane = iota((1, width), 1)

    def per_tile(values):
        result = jnp.zeros(values[0].shape, F32)
        for t in range(tiles):
            result = jnp.where(lane == t, values[t], result)
        return result.astype(BF)

    def flag(x):
        return jnp.where(x > 0, 0.0, MASKED)

    for u in range(tiles):
        bias[u * tile : (u + 1) * tile, :] = per_tile(
            [jnp.full((tile, width), flag(lmask[t, u]), F32) for t in range(tiles)]
        )
    row_c = iota((cap, width), 0)
    for side in range(2):
        start = rows + side * cap
        bias[start : start + cap, :] = per_tile(
            [
                jnp.where(row_c < live[0, side], flag(lmask[t, tiles + side]), MASKED)
                for t in range(tiles)
            ]
        )
    row_m = iota((blk, width), 0)

    def mix_mask(d):
        source = lax.rem(me + n - d, n)
        values = []
        for t in range(tiles):
            inner = jnp.where(row_m < vn + slots, flag(emask[t, source]), MASKED)
            values.append(jnp.where(row_m < vn, 0.0, inner))
        bias[pl.ds(mix0 + d * blk, blk), :] = per_tile(values)

    each(n, mix_mask)

    feature = iota((width, rows), 0)

    def blocks(x):
        parts = []
        for h in range(heads):
            mine = (feature >= h * hd) & (feature < (h + 1) * hd)
            parts.append(jnp.where(mine, x, 0.0))
        return jnp.concatenate(parts, axis=1).astype(BF)

    loads[6].wait()
    q_t = jnp.transpose(q_v[...].astype(F32)) * (hd ** -0.5)
    q_blocks = blocks(q_t)
    col = iota((width, cols), 1)
    for h in range(1, heads):
        col = jnp.where(iota((width, cols), 1) >= h * rows, iota((width, cols), 1) - h * rows, col)
    tile_of = jnp.zeros((width, cols), jnp.int32)
    for t in range(1, tiles):
        tile_of = jnp.where(col >= t * tile, t, tile_of)
    in_tile = jnp.where(iota((width, cols), 0) == tile_of, 1.0, 0.0).astype(BF)
    q_aug = jnp.concatenate([q_blocks, in_tile], axis=0)

    chunks = [(0, rows), (rows, 2 * cap)]
    step_rows = min(n * blk, 256)
    chunks += [(mix0 + i, step_rows) for i in range(0, n * blk, step_rows)]

    def score(c):
        a, size = c
        keys = jnp.concatenate([kv[a : a + size, :width], bias[a : a + size, :]], axis=1)
        s = mm(keys, q_aug, NN)
        top = jnp.max(s, axis=0, keepdims=True)
        e = jnp.exp(s - top)
        e_ref[a : a + size, :] = e
        kvt[:, a : a + size] = jnp.transpose(kv[a : a + size, :])
        return top, jnp.sum(e, axis=0, keepdims=True)

    stats = [score(chunks[0])]
    g_right = jnp.where(iota((rows, cap), 0) == hrows[0, 0:1, :], 1.0, 0.0).astype(BF)
    g_left = jnp.where(iota((rows, cap), 0) == hrows[0, 1:2, :], 1.0, 0.0).astype(BF)
    for c in halo:
        c.wait_recv()
    stats.append(score(chunks[1]))
    each(n - 1, lambda d: mix_copy(d + 1).wait_recv())
    for c in chunks[2:]:
        stats.append(score(c))

    loads[7].wait()
    for d in range(1, mp):
        cot_copy(d, lax.rem(mm_i + mp - d, mp)).wait_recv()
    g_t = mm(w_v[...], jnp.concatenate([cot[i] for i in range(mp)], axis=1), NT)
    g_t = g_t.astype(BF).astype(F32)
    g_blocks = blocks(g_t)

    top = functools.reduce(jnp.maximum, [t for t, _ in stats])
    factor = [jnp.exp(t - top) for t, _ in stats]
    norm = sum(f * z for f, (_, z) in zip(factor, stats))
    inv = 1.0 / norm
    factor = {c: f * inv for c, f in zip(chunks, factor)}
    for a, size in chunks:
        pb_ref[a : a + size, :] = (e_ref[a : a + size, :] * factor[(a, size)]).astype(BF)

    attn_t = jnp.concatenate(
        [
            mm(
                kvt[width + h * hd : width + (h + 1) * hd, :],
                pb_ref[:, h * rows : (h + 1) * rows],
                NN,
            )
            for h in range(heads)
        ],
        axis=0,
    )
    attn_t = attn_t.astype(BF).astype(F32)
    attn = jnp.transpose(attn_t).astype(BF)

    def proj_copy(d):
        peer = lax.rem(mm_i + d, mp)
        return pltpu.make_async_remote_copy(
            proj.at[peer], proj_in.at[d], proj_s.at[d], proj_r.at[d],
            device_id={"mp": peer}, device_id_type=MESH,
        )

    full = mm(attn, w_v[...], NN)
    for i in range(mp):
        proj[i] = full[:, i * width : (i + 1) * width].astype(BF)
    for d in range(1, mp):
        proj_copy(d).start()

    prod = g_t * attn_t
    delta = jnp.concatenate(
        [jnp.sum(prod[h * hd : (h + 1) * hd, :], axis=0, keepdims=True) for h in range(heads)],
        axis=1,
    )

    def backward(c):
        a, size = c
        dp = mm(kv[a : a + size, width:], g_blocks, NN)
        ds = (e_ref[a : a + size, :] * factor[c] * (dp - delta)).astype(BF)
        ds_ref[a : a + size, :] = ds
        gk = mm(ds, q_blocks, NT)
        gv = mm(pb_ref[a : a + size, :], g_blocks, NT)
        return gk, gv

    def halo_home(side):
        return pltpu.make_async_remote_copy(
            gback.at[side * cap : (side + 1) * cap, :], ret_halo.at[side],
            hb_s.at[side], hb_r.at[side],
            device_id={"nodes": left if side == 0 else right}, device_id_type=MESH,
        )

    def mix_home(d):
        return pltpu.make_async_remote_copy(
            gback.at[pl.ds(2 * cap + d * blk, blk), :], ret_mix.at[pl.ds(d * blk, blk), :],
            mb_s.at[d], mb_r.at[d],
            device_id={"nodes": lax.rem(me + n - d, n)}, device_id_type=MESH,
        )

    gk, gv = backward(chunks[1])
    gback[: 2 * cap, :width] = gk.astype(BF)
    gback[: 2 * cap, width:] = gv.astype(BF)
    home = [halo_home(0), halo_home(1)]
    for c in home:
        c.start()
    for c in chunks[2:]:
        gk, gv = backward(c)
        a = c[0] - rows
        gback[a : a + c[1], :width] = gk.astype(BF)
        gback[a : a + c[1], width:] = gv.astype(BF)
    each(n - 1, lambda d: mix_home(d + 1).start())
    gk, gv = backward(chunks[0])
    own_v[:, :width] = gk
    own_v[:, width:] = gv
    ret_mix[:blk, :] = gback[2 * cap : 2 * cap + blk, :]

    gq_t = jnp.concatenate(
        [
            mm(kvt[h * hd : (h + 1) * hd, :], ds_ref[:, h * rows : (h + 1) * rows], NN)
            for h in range(heads)
        ],
        axis=0,
    )
    gq_v[...] = jnp.transpose(gq_t * (hd ** -0.5))

    mine = mm(attn, w_v[:, pl.ds(pl.multiple_of(mm_i * width, width), width)], NN)
    for d in range(1, mp):
        proj_copy(d).wait_recv()
        mine = mine + proj_in[d].astype(F32)
    out_v[...] = mine.astype(BF)

    for c in home:
        c.wait_recv()
    acc = own_v[...] + mm(g_right, ret_halo[0], NN) + mm(g_left, ret_halo[1], NN)
    each(n - 1, lambda d: mix_home(d + 1).wait_recv())
    acc = acc + mm(onehot[...], ret_mix[...], TN)
    gk_v[...] = acc[:, :width]
    gv_v[...] = acc[:, width:]
    virt = jnp.sum(ret_mix[...].astype(F32).reshape(n, blk, 2 * width), axis=0)
    gvk_v[...] = virt[:vn, :width]
    gvv_v[...] = virt[:vn, width:]
    for c in halo + home:
        c.wait_send()
    each(n - 1, lambda d: mix_copy(d + 1).wait_send())
    each(n - 1, lambda d: mix_home(d + 1).wait_send())
    for d in range(1, mp):
        cot_copy(d, mm_i).wait_send()
        proj_copy(d).wait_send()


def hand_over(*refs):
    sem = refs[-1]
    copies = [pltpu.make_async_copy(refs[i], refs[6 + i], sem.at[i]) for i in range(6)]
    for c in copies:
        c.start()
    for c in copies:
        c.wait()


def solution(mesh):
    n, mp = mesh.shape["nodes"], mesh.shape["mp"]
    heads = HEADS // mp

    def step(q, k, v, w, cot, vk, vv, hrows, live, erows, lmask, emask):
        rows, width = q.shape
        cap, slots, vn = hrows.shape[2], erows.shape[2], vk.shape[0]
        blk = -(-(vn + slots) // 16) * 16
        total = rows + 2 * cap + n * blk
        hbm = pl.BlockSpec(memory_space=pltpu.HBM)
        anywhere = pl.BlockSpec(memory_space=pl.ANY)
        erows = jnp.swapaxes(erows, 1, 2)
        smalls = [pltpu.SMEM(x.shape, jnp.int32) for x in (live, erows, lmask, emask)]
        dma = pltpu.SemaphoreType.DMA
        flops = 2 * total * rows * width * 5
        operands = [
            pltpu.with_memory_space_constraint(x, pltpu.HBM)
            for x in (live, erows, lmask, emask, q, k, v, w, cot, vk, vv, hrows)
        ]
        results = pl.pallas_call(
            functools.partial(kernel, n, mp, heads),
            out_shape=(
                jax.ShapeDtypeStruct((rows, width), BF),
                jax.ShapeDtypeStruct((rows, width), F32),
                jax.ShapeDtypeStruct((rows, width), F32),
                jax.ShapeDtypeStruct((rows, width), F32),
                jax.ShapeDtypeStruct((vn, width), F32),
                jax.ShapeDtypeStruct((vn, width), F32),
            ),
            in_specs=[hbm] * 12,
            out_specs=(pl.BlockSpec(memory_space=pltpu.VMEM),) * 6,
            scratch_shapes=smalls + [
                pltpu.VMEM((rows, width), BF),
                pltpu.VMEM(w.shape, BF),
                pltpu.VMEM((vn, width), BF),
                pltpu.VMEM((vn, width), BF),
                pltpu.VMEM(hrows.shape, jnp.int32),
                pltpu.VMEM((total, 2 * width), BF),
                pltpu.VMEM((mp, rows, width), BF),
                pltpu.VMEM((total, width), BF),
                pltpu.VMEM((n * blk, rows), BF),
                pltpu.VMEM((n * blk, 2 * width), BF),
                pltpu.VMEM((2, cap, 2 * width), BF),
                pltpu.VMEM((2 * width, total), BF),
                pltpu.VMEM((total, heads * rows), F32),
                pltpu.VMEM((total, heads * rows), BF),
                pltpu.VMEM((total, heads * rows), BF),
                pltpu.VMEM((2 * cap + n * blk, 2 * width), BF),
                pltpu.VMEM((2, cap, 2 * width), BF),
                pltpu.VMEM((n * blk, 2 * width), BF),
                pltpu.VMEM((mp, rows, width), BF),
                pltpu.VMEM((mp, rows, width), BF),
                pltpu.VMEM((rows, 2 * width), F32),
                dma((12,)),
                dma((2,)), dma((2,)), dma((n,)), dma((n,)),
                dma((mp,)), dma((mp,)), dma((mp,)), dma((mp,)),
                dma((2,)), dma((2,)), dma((n,)), dma((n,)),
            ],
            compiler_params=pltpu.CompilerParams(
                collective_id=0, has_side_effects=True, vmem_limit_bytes=40 << 20
            ),
            cost_estimate=pl.CostEstimate(
                flops=flops, transcendentals=total * rows * heads, bytes_accessed=2 << 20
            ),
        )(*operands)
        return pl.pallas_call(
            hand_over,
            out_shape=tuple(jax.ShapeDtypeStruct(x.shape, x.dtype) for x in results),
            in_specs=[anywhere] * 6,
            out_specs=(hbm,) * 6,
            scratch_shapes=[dma((6,))],
            compiler_params=pltpu.CompilerParams(vmem_limit_bytes=4 << 20),
            cost_estimate=pl.CostEstimate(flops=0, transcendentals=0, bytes_accessed=1 << 20),
        )(*results)

    node = P("nodes", "mp")
    return jax.shard_map(
        step,
        mesh=mesh,
        in_specs=(
            node, node, node, P("mp", None), node, node, node,
            P("nodes", None, None), P("nodes", None), P("nodes", None, None),
            P("nodes", None), P("nodes", None),
        ),
        out_specs=(node,) * 6,
        check_vma=False,
    )
```

```python
import functools

import jax
import jax.numpy as jnp
from jax import lax
from jax.experimental import pallas as pl
from jax.experimental.pallas import tpu as pltpu
from jax.sharding import PartitionSpec as P

HEADS = 8
MESH = pl.DeviceIdType.MESH
BF = jnp.bfloat16
F32 = jnp.float32
MASKED = -1e30

NN = (((1,), (0,)), ((), ()))
NT = (((1,), (1,)), ((), ()))
TN = (((0,), (0,)), ((), ()))


def mm(a, b, dims):
    return lax.dot_general(a, b, dims, preferred_element_type=F32)


def iota(shape, axis):
    return lax.broadcasted_iota(jnp.int32, shape, axis)


def each(count, step):
    if count <= 8:
        for d in range(count):
            step(d)
    else:
        pl.loop(0, count)(step)


def kernel(
    n, mp, heads,
    live_hbm, erows_hbm, lmask_hbm, emask_hbm,
    q_hbm, k_hbm, v_hbm, w_hbm, cot_hbm, vk_hbm, vv_hbm, hrows_hbm,
    out_v, gq_v, gk_v, gv_v, gvk_v, gvv_v,
    live, erows, lmask, emask, q_v, w_v, vk_v, vv_v, hrows, kv, cot, bias, onehot, mix_send, halo_send,
    kvt, e_ref, pb_ref, ds_ref, gback, ret_halo, ret_mix, proj, proj_in, own_v,
    in_sem, halo_s, halo_r, mix_s, mix_r, cot_s, cot_r, proj_s, proj_r,
    hb_s, hb_r, mb_s, mb_r,
):
    me = lax.axis_index("nodes")
    mm_i = lax.axis_index("mp")
    rows, width = q_v.shape
    tiles = lmask.shape[0]
    tile = rows // tiles
    cap = hrows.shape[2]
    slots = erows.shape[1]
    vn = vk_v.shape[0]
    blk = ret_mix.shape[0] // n
    hd = width // heads
    cols = heads * rows
    left, right = lax.rem(me + n - 1, n), lax.rem(me + 1, n)
    mix0 = rows + 2 * cap
    total = mix0 + n * blk

    barrier = pltpu.get_barrier_semaphore()

    def hello(d):
        pl.semaphore_signal(
            barrier, inc=1, device_id={"nodes": lax.rem(me + d + 1, n)}, device_id_type=MESH
        )

    each(n - 1, hello)
    for d in range(1, mp):
        pl.semaphore_signal(
            barrier, inc=1, device_id={"mp": lax.rem(mm_i + d, mp)}, device_id_type=MESH
        )

    small = [
        pltpu.make_async_copy(src, dst, in_sem.at[8 + i])
        for i, (src, dst) in enumerate(
            ((erows_hbm, erows), (live_hbm, live), (lmask_hbm, lmask), (emask_hbm, emask))
        )
    ]
    for c in small:
        c.start()
    loads = [
        pltpu.make_async_copy(k_hbm, kv.at[:rows, :width], in_sem.at[0]),
        pltpu.make_async_copy(v_hbm, kv.at[:rows, width:], in_sem.at[1]),
        pltpu.make_async_copy(hrows_hbm, hrows, in_sem.at[2]),
        pltpu.make_async_copy(vk_hbm, vk_v, in_sem.at[3]),
        pltpu.make_async_copy(vv_hbm, vv_v, in_sem.at[4]),
        pltpu.make_async_copy(cot_hbm, cot.at[mm_i], in_sem.at[5]),
        pltpu.make_async_copy(q_hbm, q_v, in_sem.at[6]),
        pltpu.make_async_copy(w_hbm, w_v, in_sem.at[7]),
    ]
    for c in loads:
        c.start()

    row_b, lane_b = iota((blk, rows), 0), iota((blk, rows), 1)

    def fill(d):
        peer = lax.rem(me + d, n)
        target = jnp.full((blk, rows), -1, jnp.int32)
        for s in range(slots):
            target = jnp.where(row_b == vn + s, erows[0, s, peer], target)
        onehot[pl.ds(d * blk, blk), :] = jnp.where(lane_b == target, 1.0, 0.0).astype(BF)

    small[0].wait()
    each(n, fill)

    for c in loads[:3]:
        c.wait()
    own = kv[:rows, :]
    wanted = jnp.concatenate([hrows[0].astype(F32), jnp.zeros((6, cap), F32)], axis=0)
    wanted = jnp.transpose(wanted).astype(jnp.int32)
    wanted = jnp.concatenate([wanted[:, 0:1], wanted[:, 1:2]], axis=0)
    picks = jnp.where(iota((2 * cap, rows), 1) == wanted, 1.0, 0.0).astype(BF)
    halo_send[...] = mm(picks, own, NN).astype(BF).reshape(2, cap, 2 * width)

    for c in loads[3:5]:
        c.wait()
    virt = jnp.concatenate([vk_v[...].astype(F32), vv_v[...].astype(F32)], axis=1)
    virt = jnp.concatenate([virt, jnp.zeros((blk - vn, 2 * width), F32)], axis=0)
    taken = mm(onehot[...], own, NN).reshape(n, blk, 2 * width) + virt[None]
    taken = taken.astype(BF)
    mix_send[...] = taken.reshape(n * blk, 2 * width)

    pl.semaphore_wait(barrier, n - 1 + mp - 1)

    def halo_copy(side):
        start = rows + side * cap
        return pltpu.make_async_remote_copy(
            halo_send.at[side], kv.at[start : start + cap, :], halo_s.at[side], halo_r.at[side],
            device_id={"nodes": right if side == 0 else left}, device_id_type=MESH,
        )

    def mix_copy(d):
        return pltpu.make_async_remote_copy(
            mix_send.at[pl.ds(d * blk, blk), :], kv.at[pl.ds(mix0 + d * blk, blk), :],
            mix_s.at[d], mix_r.at[d],
            device_id={"nodes": lax.rem(me + d, n)}, device_id_type=MESH,
        )

    def cot_copy(d, slot):
        return pltpu.make_async_remote_copy(
            cot.at[slot], cot.at[slot], cot_s.at[d], cot_r.at[d],
            device_id={"mp": lax.rem(mm_i + d, mp)}, device_id_type=MESH,
        )

    each(n - 1, lambda d: mix_copy(d + 1).start())
    halo = [halo_copy(0), halo_copy(1)]
    for c in halo:
        c.start()

    loads[5].wait()
    for d in range(1, mp):
        cot_copy(d, mm_i).start()

    kv[mix0 : mix0 + blk, :] = taken[0]
    for c in small[1:]:
        c.wait()

    lane = iota((1, width), 1)

    def per_tile(values):
        result = jnp.zeros(values[0].shape, F32)
        for t in range(tiles):
            result = jnp.where(lane == t, values[t], result)
        return result.astype(BF)

    def flag(x):
        return jnp.where(x > 0, 0.0, MASKED)

    for u in range(tiles):
        bias[u * tile : (u + 1) * tile, :] = per_tile(
            [jnp.full((tile, width), flag(lmask[t, u]), F32) for t in range(tiles)]
        )
    row_c = iota((cap, width), 0)
    for side in range(2):
        start = rows + side * cap
        bias[start : start + cap, :] = per_tile(
            [
                jnp.where(row_c < live[0, side], flag(lmask[t, tiles + side]), MASKED)
                for t in range(tiles)
            ]
        )
    row_m = iota((blk, width), 0)

    def mix_mask(d):
        source = lax.rem(me + n - d, n)
        values = []
        for t in range(tiles):
            inner = jnp.where(row_m < vn + slots, flag(emask[t, source]), MASKED)
            values.append(jnp.where(row_m < vn, 0.0, inner))
        bias[pl.ds(mix0 + d * blk, blk), :] = per_tile(values)

    each(n, mix_mask)

    feature = iota((width, rows), 0)

    def blocks(x):
        parts = []
        for h in range(heads):
            mine = (feature >= h * hd) & (feature < (h + 1) * hd)
            parts.append(jnp.where(mine, x, 0.0))
        return jnp.concatenate(parts, axis=1).astype(BF)

    loads[6].wait()
    q_t = jnp.transpose(q_v[...].astype(F32)) * (hd ** -0.5)
    q_blocks = blocks(q_t)
    col = iota((width, cols), 1)
    for h in range(1, heads):
        col = jnp.where(iota((width, cols), 1) >= h * rows, iota((width, cols), 1) - h * rows, col)
    tile_of = jnp.zeros((width, cols), jnp.int32)
    for t in range(1, tiles):
        tile_of = jnp.where(col >= t * tile, t, tile_of)
    in_tile = jnp.where(iota((width, cols), 0) == tile_of, 1.0, 0.0).astype(BF)
    q_aug = jnp.concatenate([q_blocks, in_tile], axis=0)

    chunks = [(0, rows), (rows, 2 * cap)]
    step_rows = min(n * blk, 256)
    chunks += [(mix0 + i, step_rows) for i in range(0, n * blk, step_rows)]

    def score(c):
        a, size = c
        keys = jnp.concatenate([kv[a : a + size, :width], bias[a : a + size, :]], axis=1)
        s = mm(keys, q_aug, NN)
        top = jnp.max(s, axis=0, keepdims=True)
        e = jnp.exp(s - top)
        e_ref[a : a + size, :] = e
        kvt[:, a : a + size] = jnp.transpose(kv[a : a + size, :])
        return top, jnp.sum(e, axis=0, keepdims=True)

    stats = [score(chunks[0])]
    g_right = jnp.where(iota((rows, cap), 0) == hrows[0, 0:1, :], 1.0, 0.0).astype(BF)
    g_left = jnp.where(iota((rows, cap), 0) == hrows[0, 1:2, :], 1.0, 0.0).astype(BF)
    for c in halo:
        c.wait_recv()
    stats.append(score(chunks[1]))
    each(n - 1, lambda d: mix_copy(d + 1).wait_recv())
    for c in chunks[2:]:
        stats.append(score(c))

    loads[7].wait()
    for d in range(1, mp):
        cot_copy(d, lax.rem(mm_i + mp - d, mp)).wait_recv()
    g_t = mm(w_v[...], jnp.concatenate([cot[i] for i in range(mp)], axis=1), NT)
    g_t = g_t.astype(BF).astype(F32)
    g_blocks = blocks(g_t)

    top = functools.reduce(jnp.maximum, [t for t, _ in stats])
    factor = [jnp.exp(t - top) for t, _ in stats]
    norm = sum(f * z for f, (_, z) in zip(factor, stats))
    inv = 1.0 / norm
    factor = {c: f * inv for c, f in zip(chunks, factor)}
    for a, size in chunks:
        pb_ref[a : a + size, :] = (e_ref[a : a + size, :] * factor[(a, size)]).astype(BF)

    attn_t = jnp.concatenate(
        [
            mm(
                kvt[width + h * hd : width + (h + 1) * hd, :],
                pb_ref[:, h * rows : (h + 1) * rows],
                NN,
            )
            for h in range(heads)
        ],
        axis=0,
    )
    attn_t = attn_t.astype(BF).astype(F32)
    attn = jnp.transpose(attn_t).astype(BF)

    def proj_copy(d):
        peer = lax.rem(mm_i + d, mp)
        return pltpu.make_async_remote_copy(
            proj.at[peer], proj_in.at[d], proj_s.at[d], proj_r.at[d],
            device_id={"mp": peer}, device_id_type=MESH,
        )

    full = mm(attn, w_v[...], NN)
    for i in range(mp):
        proj[i] = full[:, i * width : (i + 1) * width].astype(BF)
    for d in range(1, mp):
        proj_copy(d).start()

    prod = g_t * attn_t
    delta = jnp.concatenate(
        [jnp.sum(prod[h * hd : (h + 1) * hd, :], axis=0, keepdims=True) for h in range(heads)],
        axis=1,
    )

    def backward(c):
        a, size = c
        dp = mm(kv[a : a + size, width:], g_blocks, NN)
        ds = (e_ref[a : a + size, :] * factor[c] * (dp - delta)).astype(BF)
        ds_ref[a : a + size, :] = ds
        gk = mm(ds, q_blocks, NT)
        gv = mm(pb_ref[a : a + size, :], g_blocks, NT)
        return gk, gv

    def halo_home(side):
        return pltpu.make_async_remote_copy(
            gback.at[side * cap : (side + 1) * cap, :], ret_halo.at[side],
            hb_s.at[side], hb_r.at[side],
            device_id={"nodes": left if side == 0 else right}, device_id_type=MESH,
        )

    def mix_home(d):
        return pltpu.make_async_remote_copy(
            gback.at[pl.ds(2 * cap + d * blk, blk), :], ret_mix.at[pl.ds(d * blk, blk), :],
            mb_s.at[d], mb_r.at[d],
            device_id={"nodes": lax.rem(me + n - d, n)}, device_id_type=MESH,
        )

    gk, gv = backward(chunks[1])
    gback[: 2 * cap, :width] = gk.astype(BF)
    gback[: 2 * cap, width:] = gv.astype(BF)
    home = [halo_home(0), halo_home(1)]
    for c in home:
        c.start()
    for c in chunks[2:]:
        gk, gv = backward(c)
        a = c[0] - rows
        gback[a : a + c[1], :width] = gk.astype(BF)
        gback[a : a + c[1], width:] = gv.astype(BF)
    each(n - 1, lambda d: mix_home(d + 1).start())
    gk, gv = backward(chunks[0])
    own_v[:, :width] = gk
    own_v[:, width:] = gv
    ret_mix[:blk, :] = gback[2 * cap : 2 * cap + blk, :]

    gq_t = jnp.concatenate(
        [
            mm(kvt[h * hd : (h + 1) * hd, :], ds_ref[:, h * rows : (h + 1) * rows], NN)
            for h in range(heads)
        ],
        axis=0,
    )
    gq_v[...] = jnp.transpose(gq_t * (hd ** -0.5))

    mine = mm(attn, w_v[:, pl.ds(pl.multiple_of(mm_i * width, width), width)], NN)
    for d in range(1, mp):
        proj_copy(d).wait_recv()
        mine = mine + proj_in[d].astype(F32)
    out_v[...] = mine.astype(BF)

    for c in home:
        c.wait_recv()
    acc = own_v[...] + mm(g_right, ret_halo[0], NN) + mm(g_left, ret_halo[1], NN)
    each(n - 1, lambda d: mix_home(d + 1).wait_recv())
    acc = acc + mm(onehot[...], ret_mix[...], TN)
    gk_v[...] = acc[:, :width]
    gv_v[...] = acc[:, width:]
    virt = jnp.sum(ret_mix[...].astype(F32).reshape(n, blk, 2 * width), axis=0)
    gvk_v[...] = virt[:vn, :width]
    gvv_v[...] = virt[:vn, width:]
    for c in halo + home:
        c.wait_send()
    each(n - 1, lambda d: mix_copy(d + 1).wait_send())
    each(n - 1, lambda d: mix_home(d + 1).wait_send())
    for d in range(1, mp):
        cot_copy(d, mm_i).wait_send()
        proj_copy(d).wait_send()


def hand_over(*refs):
    sem = refs[-1]
    copies = [pltpu.make_async_copy(refs[i], refs[6 + i], sem.at[i]) for i in range(6)]
    for c in copies:
        c.start()
    for c in copies:
        c.wait()


def solution(mesh):
    n, mp = mesh.shape["nodes"], mesh.shape["mp"]
    heads = HEADS // mp

    def step(q, k, v, w, cot, vk, vv, hrows, live, erows, lmask, emask):
        rows, width = q.shape
        cap, slots, vn = hrows.shape[2], erows.shape[2], vk.shape[0]
        blk = -(-(vn + slots) // 16) * 16
        total = rows + 2 * cap + n * blk
        hbm = pl.BlockSpec(memory_space=pltpu.HBM)
        anywhere = pl.BlockSpec(memory_space=pl.ANY)
        erows = jnp.swapaxes(erows, 1, 2)
        smalls = [pltpu.SMEM(x.shape, jnp.int32) for x in (live, erows, lmask, emask)]
        dma = pltpu.SemaphoreType.DMA
        flops = 2 * total * rows * width * 5
        operands = [
            pltpu.with_memory_space_constraint(x, pltpu.HBM)
            for x in (live, erows, lmask, emask, q, k, v, w, cot, vk, vv, hrows)
        ]
        results = pl.pallas_call(
            functools.partial(kernel, n, mp, heads),
            out_shape=(
                jax.ShapeDtypeStruct((rows, width), BF),
                jax.ShapeDtypeStruct((rows, width), F32),
                jax.ShapeDtypeStruct((rows, width), F32),
                jax.ShapeDtypeStruct((rows, width), F32),
                jax.ShapeDtypeStruct((vn, width), F32),
                jax.ShapeDtypeStruct((vn, width), F32),
            ),
            in_specs=[hbm] * 12,
            out_specs=(pl.BlockSpec(memory_space=pltpu.VMEM),) * 6,
            scratch_shapes=smalls + [
                pltpu.VMEM((rows, width), BF),
                pltpu.VMEM(w.shape, BF),
                pltpu.VMEM((vn, width), BF),
                pltpu.VMEM((vn, width), BF),
                pltpu.VMEM(hrows.shape, jnp.int32),
                pltpu.VMEM((total, 2 * width), BF),
                pltpu.VMEM((mp, rows, width), BF),
                pltpu.VMEM((total, width), BF),
                pltpu.VMEM((n * blk, rows), BF),
                pltpu.VMEM((n * blk, 2 * width), BF),
                pltpu.VMEM((2, cap, 2 * width), BF),
                pltpu.VMEM((2 * width, total), BF),
                pltpu.VMEM((total, heads * rows), F32),
                pltpu.VMEM((total, heads * rows), BF),
                pltpu.VMEM((total, heads * rows), BF),
                pltpu.VMEM((2 * cap + n * blk, 2 * width), BF),
                pltpu.VMEM((2, cap, 2 * width), BF),
                pltpu.VMEM((n * blk, 2 * width), BF),
                pltpu.VMEM((mp, rows, width), BF),
                pltpu.VMEM((mp, rows, width), BF),
                pltpu.VMEM((rows, 2 * width), F32),
                dma((12,)),
                dma((2,)), dma((2,)), dma((n,)), dma((n,)),
                dma((mp,)), dma((mp,)), dma((mp,)), dma((mp,)),
                dma((2,)), dma((2,)), dma((n,)), dma((n,)),
            ],
            compiler_params=pltpu.CompilerParams(
                collective_id=0, has_side_effects=True, vmem_limit_bytes=40 << 20
            ),
            cost_estimate=pl.CostEstimate(
                flops=flops, transcendentals=total * rows * heads, bytes_accessed=2 << 20
            ),
        )(*operands)
        return pl.pallas_call(
            hand_over,
            out_shape=tuple(jax.ShapeDtypeStruct(x.shape, x.dtype) for x in results),
            in_specs=[anywhere] * 6,
            out_specs=(hbm,) * 6,
            scratch_shapes=[dma((6,))],
            compiler_params=pltpu.CompilerParams(vmem_limit_bytes=4 << 20),
            cost_estimate=pl.CostEstimate(flops=0, transcendentals=0, bytes_accessed=1 << 20),
        )(*results)

    node = P("nodes", "mp")
    return jax.shard_map(
        step,
        mesh=mesh,
        in_specs=(
            node, node, node, P("mp", None), node, node, node,
            P("nodes", None, None), P("nodes", None), P("nodes", None, None),
            P("nodes", None), P("nodes", None),
        ),
        out_specs=(node,) * 6,
        check_vma=False,
    )
```
